256 devices in a mesh: tm: 32 (over x, z_hi, core), head: 8 (over z_lo, y).
Axes of the slice: x: 4, y: 4, z: 8 (z_hi: 4, z_lo: 2; z = z_hi * 2 + z_lo), core: 2. Of those that a mesh axis runs over, the one named last changes fastest.
Arguments:
- query_states: bfloat16 [49152, 1024], P('tm', 'head'), may hold values from -30 to 30
- key_states: bfloat16 [49152, 1024], P('tm', 'head'), may hold values from -30 to 30
- value_states: bfloat16 [49152, 1024], P('tm', 'head'), may hold values from -6 to 6
- win_start: int32 [64], P('tm'), may hold values from 0 to 62, as said below
- group_end: int32 [64], P('tm'), may hold values from 0 to 63, as said below
- out_weight: bfloat16 [1024, 1536], replicated, may hold values from -0.1875 to 0.1875
Outputs:
- projected: bfloat16 [49152, 1536], P(('tm', 'head'))
The draws below stay inside these ranges and needn't reach their ends.
Inputs may be any that keep to these rules, and one draw needn't show every extreme that they name: For every frame f, win_start[f] = max(f - lag, 0) with a lag of 1 to 3; frame 64 - 2 has a lag of 3 in every draw, and the last frame has a lag of 1. `group_end`: frames 2p and 2p + 1 form one group (both end at 2p + 1) or two groups of one frame (each ends at itself); both kinds occur in every draw.
All inputs are finite; a program needn't handle non-finite values.
Results may differ from the reference program's by a relative error of at most 0.0051.
Values may be sent and summed in bfloat16 or wider, within the bound.
A program may use at most 64 MiB of HBM per device.

```python
import jax
import jax.numpy as jnp
from jax import lax

D = 1536
HEADS = 8
HD = 128
FT = 768
NF = 64
TOKENS = 49152


def paired_states(key):
    width = HEADS * HD
    key_base = jax.random.fold_in(key, 11)
    query_base = jax.random.fold_in(key, 12)
    key_draw = jnp.clip(2.0 * jax.random.normal(key_base, (TOKENS, width), jnp.float32), -12.0, 12.0)
    query_draw = jnp.clip(2.0 * jax.random.normal(query_base, (TOKENS, width), jnp.float32), -12.0, 12.0)
    return (query_draw, key_draw)


def draw_query_states(key, part):
    return paired_states(key)[0].astype(jnp.bfloat16)


def draw_key_states(key, part):
    return paired_states(key)[1].astype(jnp.bfloat16)


def draw_win_start(key, part):
    frame = jnp.arange(NF, dtype=jnp.int32)
    lagged = jax.random.randint(jax.random.fold_in(key, 21), (NF,), 1, 4, dtype=jnp.int32)
    lagged = jnp.where(frame % 8 == 5, 3, lagged)
    lagged = jnp.where(frame == NF - 2, 3, lagged)
    lagged = jnp.where(frame == NF - 1, 1, lagged)
    return jnp.maximum(frame - lagged, 0).astype(jnp.int32)


def draw_group_end(key, part):
    frame = jnp.arange(NF, dtype=jnp.int32)
    paired = frame // 2
    joined = jax.random.randint(jax.random.fold_in(key, 22), (NF // 2,), 0, 2, dtype=jnp.int32)
    joined = jnp.where(jnp.arange(NF // 2) % 4 == 1, 1, jnp.where(jnp.arange(NF // 2) % 4 == 3, 0, joined))
    joined_frame = joined[paired]
    return jnp.where(joined_frame == 1, 2 * paired + 1, frame).astype(jnp.int32)


def block_levels(own_key, extent, split, low, top_value):
    level = 1.0
    for dim, shards_of in split:
        draws = jax.random.uniform(jax.random.fold_in(jax.random.fold_in(own_key, 6), dim), (shards_of,), jnp.float32, low / len(split), top_value / len(split))
        level = level * jnp.repeat(jnp.exp(draws), extent[dim] // shards_of).reshape((-1,) + (1,) * (len(extent) - 1 - dim))
    return level


def scatter_about(own_key, extent, scale, reach, pieces=(), held_as=jnp.bfloat16):
    level = block_levels(own_key, extent, pieces, -0.22, 0.18) if pieces else 1.0
    array = jax.random.normal(own_key, extent, jnp.float32) * scale * level
    return jnp.minimum(jnp.maximum(array, -reach), reach).astype(held_as)


def setup_inputs(seed: int = 0) -> dict:
    key_list = jax.random.split(jax.random.key(seed), 7)
    return {
        "query_states": draw_query_states(jax.random.fold_in(key_list[6], 71), 0),
        "key_states": draw_key_states(jax.random.fold_in(key_list[6], 71), 0),
        "value_states": scatter_about(key_list[2], (TOKENS, HEADS * HD), 1.0, 6.0, ((0, 32), (1, 8))),
        "win_start": draw_win_start(jax.random.fold_in(key_list[6], 71), 0),
        "group_end": draw_group_end(jax.random.fold_in(key_list[6], 71), 0),
        "out_weight": scatter_about(key_list[5], (HEADS * HD, D), (HEADS * HD) ** -0.5, 0.1875),
    }


def reference(query_states, key_states, value_states, win_start, group_end, out_weight):
    width = HEADS * HD
    scale = HD ** -0.5
    padding = jnp.zeros((3 * FT, width), key_states.dtype)
    tail_pad = jnp.zeros((FT, width), key_states.dtype)
    padded_keys = jnp.concatenate([padding, key_states, tail_pad], axis=0)
    padded_values = jnp.concatenate([padding, value_states, tail_pad], axis=0)
    sink_keys = key_states[:FT]
    sink_values = value_states[:FT]

    def one_frame(frame):
        query_rows = lax.dynamic_slice_in_dim(query_states, (frame * FT).astype(jnp.int32), FT, 0)
        window_keys = lax.dynamic_slice_in_dim(padded_keys, (frame * FT).astype(jnp.int32), 5 * FT, 0)
        window_values = lax.dynamic_slice_in_dim(padded_values, (frame * FT).astype(jnp.int32), 5 * FT, 0)
        all_keys = jnp.concatenate([sink_keys, window_keys], axis=0)
        all_values = jnp.concatenate([sink_values, window_values], axis=0)
        frame_ids = frame - 3 + jnp.arange(5 * FT, dtype=jnp.int32) // FT
        window_seen = (frame_ids >= 1) & (frame_ids >= win_start[frame]) & (frame_ids <= group_end[frame])
        visible = jnp.concatenate([jnp.ones((FT,), dtype=bool), window_seen])
        query_heads = query_rows.reshape(FT, HEADS, HD).astype(jnp.float32)
        key_heads = all_keys.reshape(6 * FT, HEADS, HD).astype(jnp.float32)
        value_heads = all_values.reshape(6 * FT, HEADS, HD).astype(jnp.float32)
        scores = jnp.einsum("qhd,khd->hqk", query_heads, key_heads) * scale
        scores = jnp.where(visible[None, None, :], scores, -1e30)
        peak = jnp.max(scores, axis=-1, keepdims=True)
        weights = jnp.where(visible[None, None, :], jnp.exp(scores - peak), 0.0)
        total = jnp.sum(weights, axis=-1)
        rounded = lax.optimization_barrier(weights.astype(jnp.bfloat16))
        mixed = jnp.einsum("hqk,khd->qhd", rounded.astype(jnp.float32), value_heads)
        mixed = mixed / jnp.transpose(total)[:, :, None]
        return mixed.astype(jnp.bfloat16).reshape(FT, width)

    attended = lax.map(one_frame, jnp.arange(NF, dtype=jnp.int32)).reshape(TOKENS, width)
    return jnp.dot(attended, out_weight, preferred_element_type=jnp.float32).astype(jnp.bfloat16)
```

```python
import jax
import jax.numpy as jnp
from jax import lax
from jax.experimental import pallas as pl
from jax.experimental.pallas import tpu as pltpu
from jax.sharding import PartitionSpec as P

HD = 128
FT = 768
BLK = 192
C = HD**-0.5 * 1.4426950408889634
HIDE = -1.0e6
LOW = -3.0e6
MESH = pl.DeviceIdType.MESH

Q0 = (0, 1, 0, 1, 2, 2, 3, 0, 1, 0, 1)
K0 = (0, 0, 1, 1, 1, 2, 2, 4, 4, 5, 5)
Q1 = (0, 1, 0, 1, 0, 1, 0, 1, 1, 0, 0)
K1 = (0, 0, 1, 1, 2, 2, 3, 3, 5, 5, 4)

PK0, PV0, PK1, PV1, TK, TV, RQ0, RQ1, RB, RO, RT, SK, SV, RH = (
    0, 1, 2, 3, 4, 5, 6, 7, 8, 9, 11, 13, 17, 21)
S1S, S2S, S3S, SH = 13, 19, 25, 39


def kernel(q_hbm, k_hbm, v_hbm, ws, ge, out_ref, qb, kb, vb, acc, mm, s0, s1, x0, x1,
           bt, bs, att, ro, rs, reto, rets, gath, lsem, ssem, rsem):
    tm = lax.axis_index("tm")
    hd = lax.axis_index("head")
    core = lax.rem(tm, 2)
    c = lax.div(tm, 2)
    x = lax.div(c, 4)
    zh = lax.rem(c, 4)
    other = tm + 1 - 2 * core
    has_prev = c > 0
    has_next = c < 15
    first = (c == 0).astype(jnp.int32)
    last = (c == 15).astype(jnp.int32)
    is0 = core == 0
    is1 = core == 1

    def both(*conds):
        r = conds[0]
        for d in conds[1:]:
            r = jnp.logical_and(r, d)
        return r

    def rc(src, dst, si, ri, t, h):
        return pltpu.make_async_remote_copy(
            src_ref=src, dst_ref=dst, send_sem=ssem.at[si], recv_sem=rsem.at[ri],
            device_id=(t, h), device_id_type=MESH)

    def got(dst, ri):
        rc(dst, dst, 0, ri, other, hd).wait_recv()

    def sent(src, si):
        rc(src, src, si, 0, other, hd).wait_send()

    def kf(n):
        return kb.at[pl.ds(n * FT, FT)]

    def vf(n):
        return vb.at[pl.ds(n * FT, FT), pl.ds(0, HD)]

    def kp(p):
        return kb.at[pl.ds(pl.multiple_of(5 * FT + p * BLK, BLK), BLK)]

    def vp(p):
        return vb.at[pl.ds(pl.multiple_of(5 * FT + p * BLK, BLK), BLK), pl.ds(0, HD)]

    barrier = pltpu.get_barrier_semaphore()

    def hello(t, h):
        pl.semaphore_signal(barrier, inc=1, device_id=(t, h), device_id_type=MESH)

    vb[:, HD:] = jnp.ones((6 * FT, HD), jnp.bfloat16)

    hello(other, hd)
    for d in range(1, 8):
        hello(tm, lax.rem(hd + d, 8))
    for d in range(1, 4):
        hello(2 * (lax.rem(x + d, 4) * 4 + zh), hd)

    @pl.when(both(is0, has_prev))
    def _():
        hello(tm - 2, hd)
        hello(tm - 1, hd)

    @pl.when(both(is0, has_next))
    def _():
        hello(tm + 2, hd)

    @pl.when(both(is0, zh > 0))
    def _():
        hello(2 * x * 4, hd)

    own = (
        pltpu.make_async_copy(q_hbm, qb.at[pl.ds(0, 2 * FT)], lsem.at[0]),
        pltpu.make_async_copy(k_hbm, kb.at[pl.ds(0, 2 * FT)], lsem.at[1]),
        pltpu.make_async_copy(v_hbm, vb.at[pl.ds(0, 2 * FT), pl.ds(0, HD)], lsem.at[2]),
    )
    for cp in own:
        cp.start()
    root = both(is0, c == 0)
    sink_k = pltpu.make_async_copy(k_hbm.at[pl.ds(0, BLK)], kp(0), lsem.at[3])
    sink_v = pltpu.make_async_copy(v_hbm.at[pl.ds(0, BLK)], vp(0), lsem.at[4])

    @pl.when(root)
    def _():
        sink_k.start()
        sink_v.start()

    def bias(slot, frame):
        seen = jnp.logical_and(frame >= 1, jnp.logical_and(frame >= ws[slot], frame <= ge[slot]))
        return jnp.full((8, HD), jnp.where(seen, 0.0, HIDE), jnp.float32)

    base = 2 * tm
    part = 2 * other
    for s in range(2):
        bt[s * 6 + 0] = bias(s, base)
        bt[s * 6 + 1] = bias(s, base + 1)
        bt[s * 6 + 2] = bias(s, part)
        bt[s * 6 + 3] = bias(s, part + 1)
        bt[s * 6 + 4] = bias(s, 4 * c - 1)
        bt[s * 6 + 5] = jnp.zeros((8, HD), jnp.float32)
    for s in range(2):
        for m in range(2):
            bs[2 * s + m] = bias(s, 4 * c - 3 + m)

    mm[...] = jnp.full_like(mm, LOW)
    acc[...] = jnp.zeros_like(acc)
    more = 7 - first - last + 3 * (zh == 0).astype(jnp.int32) + 1
    pl.semaphore_wait(barrier, 8 + (1 - core) * more + core * (1 - last))

    par = [
        rc(k_hbm.at[pl.ds(0, FT)], kf(2), PK0, PK0, other, hd),
        rc(v_hbm.at[pl.ds(0, FT)], vf(2), PV0, PV0, other, hd),
        rc(k_hbm.at[pl.ds(FT, FT)], kf(3), PK1, PK1, other, hd),
        rc(v_hbm.at[pl.ds(FT, FT)], vf(3), PV1, PV1, other, hd),
    ]
    send_q = [
        rc(q_hbm.at[pl.ds(0, FT)], qb.at[pl.ds(2 * FT, FT)], RQ0, RQ0, tm - 2, hd),
        rc(bs, bt.at[pl.ds(12, 4)], RB, RB, tm - 2, hd),
        rc(q_hbm.at[pl.ds(FT, FT)], qb.at[pl.ds(3 * FT, FT)], RQ1, RQ1, tm - 2, hd),
    ]
    send_t = [
        rc(k_hbm.at[pl.ds(FT, FT)], kf(4), TK, TK, tm + 1, hd),
        rc(v_hbm.at[pl.ds(FT, FT)], vf(4), TV, TV, tm + 1, hd),
    ]

    @pl.when(both(is0, has_prev))
    def _():
        for cp in send_q:
            cp.start()

    @pl.when(both(is1, has_next))
    def _():
        for cp in send_t:
            cp.start()

    stage1 = []
    for d in range(1, 4):
        stage1.append(rc(k_hbm.at[pl.ds(d * BLK, BLK)], kp(d), S1S + 2 * d - 2, SK + d, 8 * d, hd))
        stage1.append(rc(v_hbm.at[pl.ds(d * BLK, BLK)], vp(d), S1S + 2 * d - 1, SV + d, 8 * d, hd))

    @pl.when(root)
    def _():
        for cp in stage1:
            cp.start()

    for cp in par[:2]:
        cp.start()

    @pl.when(is0)
    def _():
        for cp in par[2:]:
            cp.start()

    stage2 = []
    for d in range(1, 4):
        t = 2 * (x * 4 + d)
        stage2.append(rc(kp(x), kp(x), S2S + 2 * d - 2, SK + x, t, hd))
        stage2.append(rc(vp(x), vp(x), S2S + 2 * d - 1, SV + x, t, hd))
    stage3 = []
    n = S3S
    for d in range(4):
        for e in range(2):
            if d == 0 and e == 0:
                continue
            t = 2 * (lax.rem(x + d, 4) * 4 + zh) + e
            stage3.append(rc(kp(x), kp(x), n, SK + x, t, hd))
            stage3.append(rc(vp(x), vp(x), n + 1, SV + x, t, hd))
            n += 2

    for cp in own:
        cp.wait()

    @pl.when(root)
    def _():
        sink_k.wait()
        sink_v.wait()
        for cp in stage2:
            cp.start()

    def pick(i, a, b):
        r = a[0] + core * (b[0] - a[0])
        for m in range(1, len(a)):
            r = jnp.where(i == m, a[m] + core * (b[m] - a[m]), r)
        return r

    def item(i):
        qs = pick(i, Q0, Q1)
        ks = pick(i, K0, K1)
        qd = qs - 2 * last * lax.div(qs, 2)
        kd = ks - 4 * first * (lax.div(ks, 4) - lax.div(ks, 5))
        far = lax.div(qs, 2)
        bi = (1 - far) * (qs * 6 + ks) + far * (12 + (qs - 2) * 2 + ks - 1)
        return (pl.multiple_of(qs * FT, FT), pl.multiple_of(qd * FT, FT),
                pl.multiple_of(kd * FT, FT), bi)

    def scores(i, s_ref, x_ref):
        _, qd, kd, bi = item(i)
        s = lax.dot_general(qb[pl.ds(qd, FT), :], kb[pl.ds(kd, FT), :],
                            (((1,), (1,)), ((), ())), preferred_element_type=jnp.float32)
        s_ref[...] = s
        t = s[:, :HD]
        for l in range(HD, FT, HD):
            t = jnp.maximum(t, s[:, l:l + HD])
        top = jnp.broadcast_to(jnp.max(t, axis=1, keepdims=True), (FT, HD))
        x_ref[...] = top + bt[bi][0:1]

    def mix(i, s_ref, x_ref):
        qs, _, kd, bi = item(i)
        rows = pl.ds(qs, FT)
        old = mm[rows, :]
        new = jnp.maximum(old, x_ref[...])
        keep = jnp.exp2((old - new) * C)
        mm[rows, :] = new
        sub = new - bt[bi][0:1]
        w = [jnp.exp2((s_ref[:, l:l + HD] - sub) * C).astype(jnp.bfloat16)
             for l in range(0, FT, HD)]
        d = jnp.dot(jnp.concatenate(w, axis=1), vb[pl.ds(kd, FT), :],
                    preferred_element_type=jnp.float32)
        acc[rows, :HD] = acc[rows, :HD] * keep + d[:, :HD]
        acc[rows, HD:] = acc[rows, HD:] * keep + d[:, HD:]

    def run(start, count, mid):
        scores(start, s0, x0)

        def body(h, carry):
            i = start + 2 * h
            scores(i + 1, s1, x1)
            mix(i, s0, x0)
            mid(h)
            scores(jnp.minimum(i + 2, start + count - 1), s0, x0)
            mix(i + 1, s1, x1)
            return carry

        lax.fori_loop(0, count // 2, body, 0)

    def mid_a(h):
        @pl.when(both(is0, has_next, h == 1))
        def _():
            got(qb.at[pl.ds(2 * FT, FT)], RQ0)
            got(bt.at[pl.ds(12, 4)], RB)

        @pl.when(h == 1)
        def _():
            got(kf(2), PK0)
            got(vf(2), PV0)

        @pl.when(both(is0, zh == 0, x > 0, h == 1))
        def _():
            got(kp(x), SK + x)
            got(vp(x), SV + x)
            for cp in stage2:
                cp.start()

    run(0, 6, mid_a)

    eye = (lax.broadcasted_iota(jnp.int32, (HD, HD), 0)
           == lax.broadcasted_iota(jnp.int32, (HD, HD), 1))

    def give_back(s):
        def body(b, carry):
            r = pl.multiple_of((2 + s) * FT + b * HD, HD)
            o = pl.multiple_of(s * FT + b * HD, HD)
            den = acc[pl.ds(r, HD), HD:]
            ro[pl.ds(o, HD), :] = (acc[pl.ds(r, HD), :HD] / den).astype(jnp.bfloat16)
            lse = mm[pl.ds(r, HD), :] + jnp.log2(den) * (1.0 / C)
            rs[s * 6 + b] = jnp.broadcast_to(
                jnp.sum(jnp.where(eye, lse, 0.0), axis=0, keepdims=True), (8, HD))
            return carry

        lax.fori_loop(0, 6, body, 0)

    def returns(s):
        return (rc(ro.at[pl.ds(s * FT, FT)], reto.at[pl.ds(s * FT, FT)], RO + s, RO + s, tm + 2, hd),
                rc(rs.at[pl.ds(s * 6, 6)], rets.at[pl.ds(s * 6, 6)], RT + s, RT + s, tm + 2, hd))

    @pl.when(both(is0, has_next))
    def _():
        give_back(0)
        for cp in returns(0):
            cp.start()

    @pl.when(is0)
    def _():
        @pl.when(zh > 0)
        def _():
            got(kp(x), SK + x)
            got(vp(x), SV + x)

        for cp in stage3:
            cp.start()

    @pl.when(both(is0, has_next))
    def _():
        got(qb.at[pl.ds(3 * FT, FT)], RQ1)

    @pl.when(is1)
    def _():
        got(kf(3), PK1)
        got(vf(3), PV1)

    scores(6, s1, x1)
    mix(6, s1, x1)

    relay = (rc(kf(4), kf(4), TK, TK, other, hd), rc(vf(4), vf(4), TV, TV, other, hd))

    @pl.when(both(is0, has_next))
    def _():
        give_back(1)
        for cp in returns(1):
            cp.start()

    @pl.when(both(is0, has_prev))
    def _():
        got(kf(4), TK)
        got(vf(4), TV)
        for cp in relay:
            cp.start()

    def sink_in():
        for p in range(4):
            @pl.when(jnp.logical_or(is1, x != p))
            def _():
                got(kp(p), SK + p)
                got(vp(p), SV + p)

    @pl.when(is1)
    def _():
        sink_in()

    def mid_b(h):
        @pl.when(both(is0, h == 0))
        def _():
            sink_in()

        @pl.when(both(is1, has_prev, h == 0))
        def _():
            got(kf(4), TK)
            got(vf(4), TV)

    run(7, 4, mid_b)

    def finish(s):
        merged = both(is0, has_prev)

        @pl.when(merged)
        def _():
            got(reto.at[pl.ds(s * FT, FT)], RO + s)
            got(rets.at[pl.ds(s * 6, 6)], RT + s)

            def body(b, carry):
                r = pl.multiple_of(s * FT + b * HD, HD)
                row = jnp.broadcast_to(rets[s * 6 + b][0:1], (HD, HD))
                far = jnp.broadcast_to(
                    jnp.sum(jnp.where(eye, row, 0.0), axis=1, keepdims=True), (HD, HD))
                old = mm[pl.ds(r, HD), :]
                new = jnp.maximum(old, far)
                a = jnp.exp2((old - new) * C)
                b2 = jnp.exp2((far - new) * C)
                num = acc[pl.ds(r, HD), :HD] * a + reto[pl.ds(r, HD), :].astype(jnp.float32) * b2
                den = acc[pl.ds(r, HD), HD:] * a + b2
                att[pl.ds(r, HD), :] = (num / den).astype(jnp.bfloat16)
                return carry

            lax.fori_loop(0, 6, body, 0)

        @pl.when(jnp.logical_not(merged))
        def _():
            def body(b, carry):
                r = pl.multiple_of(s * FT + b * HD, HD)
                att[pl.ds(r, HD), :] = (acc[pl.ds(r, HD), :HD] / acc[pl.ds(r, HD), HD:]).astype(jnp.bfloat16)
                return carry

            lax.fori_loop(0, 6, body, 0)

    def block(j):
        return rc(att.at[pl.ds(j * BLK, BLK)], gath.at[hd], SH + j, RH + hd, tm, j)

    for s in range(2):
        finish(s)
        for j in range(4 * s, 4 * s + 4):
            @pl.when(j != hd)
            def _():
                block(j).start()

            @pl.when(j == hd)
            def _():
                gath[hd] = att[pl.ds(j * BLK, BLK), :]

    for e in range(8):
        @pl.when(e != hd)
        def _():
            got(gath.at[e], RH + e)
        out_ref[:, e * HD:(e + 1) * HD] = gath[e]

    for cp in par[:2]:
        cp.wait_send()

    @pl.when(is0)
    def _():
        for cp in par[2:]:
            cp.wait_send()
        for cp in stage3:
            cp.wait_send()

    @pl.when(both(is0, has_prev))
    def _():
        for cp in send_q:
            cp.wait_send()
        for cp in relay:
            cp.wait_send()

    @pl.when(both(is0, has_next))
    def _():
        for s in range(2):
            for cp in returns(s):
                cp.wait_send()

    @pl.when(both(is1, has_next))
    def _():
        for cp in send_t:
            cp.wait_send()

    @pl.when(root)
    def _():
        for cp in stage1:
            cp.wait_send()

    @pl.when(both(is0, zh == 0))
    def _():
        for cp in stage2:
            cp.wait_send()

    for j in range(8):
        @pl.when(j != hd)
        def _():
            block(j).wait_send()


def local(query_states, key_states, value_states, win_start, group_end, out_weight):
    rows = pl.pallas_call(
        kernel,
        out_shape=jax.ShapeDtypeStruct((BLK, 8 * HD), jnp.bfloat16),
        in_specs=[pl.BlockSpec(memory_space=pl.ANY)] * 3 + [pl.BlockSpec(memory_space=pltpu.SMEM)] * 2,
        out_specs=pl.BlockSpec(memory_space=pltpu.VMEM),
        scratch_shapes=[
            pltpu.VMEM((4 * FT, HD), jnp.bfloat16),
            pltpu.VMEM((6 * FT, HD), jnp.bfloat16),
            pltpu.VMEM((6 * FT, 2 * HD), jnp.bfloat16),
            pltpu.VMEM((4 * FT, 2 * HD), jnp.float32),
            pltpu.VMEM((4 * FT, HD), jnp.float32),
            pltpu.VMEM((FT, FT), jnp.float32),
            pltpu.VMEM((FT, FT), jnp.float32),
            pltpu.VMEM((FT, HD), jnp.float32),
            pltpu.VMEM((FT, HD), jnp.float32),
            pltpu.VMEM((16, 8, HD), jnp.float32),
            pltpu.VMEM((4, 8, HD), jnp.float32),
            pltpu.VMEM((2 * FT, HD), jnp.bfloat16),
            pltpu.VMEM((2 * FT, HD), jnp.bfloat16),
            pltpu.VMEM((12, 8, HD), jnp.float32),
            pltpu.VMEM((2 * FT, HD), jnp.bfloat16),
            pltpu.VMEM((12, 8, HD), jnp.float32),
            pltpu.VMEM((8, BLK, HD), jnp.bfloat16),
            pltpu.SemaphoreType.DMA((5,)),
            pltpu.SemaphoreType.DMA((47,)),
            pltpu.SemaphoreType.DMA((29,)),
        ],
        compiler_params=pltpu.CompilerParams(
            collective_id=0, has_side_effects=True, vmem_limit_bytes=60 * 1024 * 1024),
        name="attend",
    )(query_states, key_states, value_states, win_start, group_end)
    return jnp.dot(rows, out_weight, preferred_element_type=jnp.float32).astype(jnp.bfloat16)


def solution(mesh):
    in_specs = (P("tm", "head"), P("tm", "head"), P("tm", "head"), P("tm"), P("tm"), P())
    out_specs = P(("tm", "head"), None)
    return jax.shard_map(local, mesh=mesh, in_specs=in_specs, out_specs=out_specs, check_vma=False)
```

```python
import jax
import jax.numpy as jnp
from jax import lax
from jax.experimental import pallas as pl
from jax.experimental.pallas import tpu as pltpu
from jax.sharding import PartitionSpec as P

HD = 128
FT = 768
BLK = 192
C = HD**-0.5 * 1.4426950408889634
HIDE = -1.0e6
LOW = -3.0e6
MESH = pl.DeviceIdType.MESH

Q0 = (0, 1, 0, 1, 2, 2, 0, 1, 3, 0, 1)
K0 = (0, 0, 1, 1, 1, 2, 4, 4, 2, 5, 5)
Q1 = (0, 1, 0, 1, 0, 1, 0, 1, 0, 0, 1)
K1 = (0, 0, 1, 1, 2, 2, 3, 3, 4, 5, 5)

PK0, PV0, PK1, PV1, TK, TV, RQ0, RQ1, RB, RO, RT, SP, SF, RH = (
    0, 1, 2, 3, 4, 5, 6, 7, 8, 9, 11, 13, 17, 18)
S1S, S2S, S3S, S4S, SH = 13, 20, 23, 26, 27


def kernel(q_hbm, k_hbm, v_hbm, ws_hbm, ge_hbm, out_ref, ws, ge, qb, kb, vb, acc, mm, s0, x0,
           bt, bs, att, ro, rs, reto, rets, gath, lsem, ssem, rsem):
    tm = lax.axis_index("tm")
    hd = lax.axis_index("head")
    core = lax.rem(tm, 2)
    c = lax.div(tm, 2)
    x = lax.div(c, 4)
    zh = lax.rem(c, 4)
    other = tm + 1 - 2 * core
    has_prev = c > 0
    has_next = c < 15
    first = (c == 0).astype(jnp.int32)
    last = (c == 15).astype(jnp.int32)
    is0 = core == 0
    is1 = core == 1

    def both(*conds):
        r = conds[0]
        for d in conds[1:]:
            r = jnp.logical_and(r, d)
        return r

    def rc(src, dst, si, ri, t, h):
        return pltpu.make_async_remote_copy(
            src_ref=src, dst_ref=dst, send_sem=ssem.at[si], recv_sem=rsem.at[ri],
            device_id=(t, h), device_id_type=MESH)

    def got(dst, ri):
        rc(dst, dst, 0, ri, other, hd).wait_recv()

    def sent(src, si):
        rc(src, src, si, 0, other, hd).wait_send()

    def kf(n):
        return kb.at[pl.ds(n * FT, FT)]

    def vf(n):
        return vb.at[pl.ds(n * FT, FT), pl.ds(0, HD)]

    def kp(p):
        return kb.at[pl.ds(pl.multiple_of(5 * FT + p * BLK, BLK), BLK)]

    def vp(p):
        return vb.at[pl.ds(pl.multiple_of(5 * FT + p * BLK, BLK), BLK), pl.ds(0, HD)]

    barrier = pltpu.get_barrier_semaphore()

    def hello(t, h):
        pl.semaphore_signal(barrier, inc=1, device_id=(t, h), device_id_type=MESH)

    own = (
        pltpu.make_async_copy(q_hbm, qb.at[pl.ds(0, 2 * FT)], lsem.at[0]),
        pltpu.make_async_copy(k_hbm, kb.at[pl.ds(0, 2 * FT)], lsem.at[1]),
        pltpu.make_async_copy(v_hbm, vb.at[pl.ds(0, 2 * FT), pl.ds(0, HD)], lsem.at[2]),
    )
    for cp in own:
        cp.start()
    limits = (pltpu.make_async_copy(ws_hbm, ws, lsem.at[4]), pltpu.make_async_copy(ge_hbm, ge, lsem.at[5]))
    for cp in limits:
        cp.start()

    vb[:, HD:] = jnp.ones((6 * FT, HD), jnp.bfloat16)

    hello(other, hd)
    for d in range(1, 8):
        hello(tm, lax.rem(hd + d, 8))
    for d in range(1, 4):
        hello(2 * (lax.rem(x + d, 4) * 4 + zh) + core, hd)

    @pl.when(both(is0, has_prev))
    def _():
        hello(tm - 2, hd)
        hello(tm - 1, hd)

    @pl.when(both(is0, has_next))
    def _():
        hello(tm + 2, hd)

    @pl.when(zh > 0)
    def _():
        hello(8 * x + core, hd)

    @pl.when(both(is1, zh == 0, x > 0))
    def _():
        hello(0, hd)

    root = both(is0, c == 0)
    sink_k = pltpu.make_async_copy(k_hbm.at[pl.ds(0, BLK)], kp(0), lsem.at[3])

    @pl.when(root)
    def _():
        sink_k.start()

    def bias(slot, frame):
        seen = jnp.logical_and(frame >= 1, jnp.logical_and(frame >= ws[slot], frame <= ge[slot]))
        return jnp.full((8, HD), jnp.where(seen, 0.0, HIDE), jnp.float32)

    for cp in limits:
        cp.wait()
    base = 2 * tm
    part = 2 * other
    for s in range(2):
        bt[s * 6 + 0] = bias(s, base)
        bt[s * 6 + 1] = bias(s, base + 1)
        bt[s * 6 + 2] = bias(s, part)
        bt[s * 6 + 3] = bias(s, part + 1)
        bt[s * 6 + 4] = bias(s, 4 * c - 1)
        bt[s * 6 + 5] = jnp.zeros((8, HD), jnp.float32)
    for s in range(2):
        for m in range(2):
            bs[2 * s + m] = bias(s, 4 * c - 3 + m)

    low = (zh == 0).astype(jnp.int32)
    head0 = first * (1 - core)
    pl.semaphore_wait(barrier, 11 + 3 * low + 3 * head0 + (1 - core) * (2 - first - last) + core * (1 - last))

    par = [
        rc(k_hbm.at[pl.ds(0, FT)], kf(2), PK0, PK0, other, hd),
        rc(v_hbm.at[pl.ds(0, FT)], vf(2), PV0, PV0, other, hd),
        rc(k_hbm.at[pl.ds(FT, FT)], kf(3), PK1, PK1, other, hd),
        rc(v_hbm.at[pl.ds(FT, FT)], vf(3), PV1, PV1, other, hd),
    ]
    send_q = [
        rc(q_hbm.at[pl.ds(0, FT)], qb.at[pl.ds(2 * FT, FT)], RQ0, RQ0, tm - 2, hd),
        rc(bs, bt.at[pl.ds(12, 4)], RB, RB, tm - 2, hd),
        rc(q_hbm.at[pl.ds(FT, FT)], qb.at[pl.ds(3 * FT, FT)], RQ1, RQ1, tm - 2, hd),
    ]
    send_t = [
        rc(k_hbm.at[pl.ds(FT, FT)], kf(4), TK, TK, tm + 1, hd),
        rc(v_hbm.at[pl.ds(FT, FT)], vf(4), TV, TV, tm + 1, hd),
    ]

    @pl.when(both(is0, has_prev))
    def _():
        send_q[0].start()
        send_q[1].start()

    @pl.when(both(is1, has_next))
    def _():
        for cp in send_t:
            cp.start()

    stage1 = [rc(v_hbm.at[pl.ds(0, BLK)], vp(0), S1S, SP, 1, hd)]
    for d in range(1, 4):
        stage1.append(rc(k_hbm.at[pl.ds(d * BLK, BLK)], kp(d), S1S + 2 * d - 1, SP + d, 8 * d, hd))
        stage1.append(rc(v_hbm.at[pl.ds(d * BLK, BLK)], vp(d), S1S + 2 * d, SP + d, 8 * d + 1, hd))

    @pl.when(root)
    def _():
        for cp in stage1:
            cp.start()

    for cp in par[:2]:
        cp.start()

    @pl.when(is0)
    def _():
        for cp in par[2:]:
            cp.start()

    def by_core(f):
        @pl.when(is0)
        def _():
            f(kp, kf)

        @pl.when(is1)
        def _():
            f(vp, vf)

    def stage2(piece):
        return [rc(piece(x), piece(x), S2S + d - 1, SP + x, 2 * (x * 4 + d) + core, hd)
                for d in range(1, 4)]

    def stage3(piece):
        return [rc(piece(x), piece(x), S3S + d - 1, SP + x,
                   2 * (lax.rem(x + d, 4) * 4 + zh) + core, hd) for d in range(1, 4)]

    def stage4(full):
        return rc(full(5), full(5), S4S, SF, other, hd)

    mm[...] = jnp.full_like(mm, LOW)
    acc[...] = jnp.zeros_like(acc)

    for cp in own:
        cp.wait()

    @pl.when(root)
    def _():
        sink_k.wait()

    def pick(i, a, b):
        r = a[0] + core * (b[0] - a[0])
        for m in range(1, len(a)):
            r = jnp.where(i == m, a[m] + core * (b[m] - a[m]), r)
        return r

    def item(i):
        qs = pick(i, Q0, Q1)
        ks = pick(i, K0, K1)
        qd = qs - 2 * last * lax.div(qs, 2)
        kd = ks - 4 * first * (lax.div(ks, 4) - lax.div(ks, 5))
        far = lax.div(qs, 2)
        bi = (1 - far) * (qs * 6 + ks) + far * (12 + (qs - 2) * 2 + ks - 1)
        return (pl.multiple_of(qs * FT, FT), pl.multiple_of(qd * FT, FT),
                pl.multiple_of(kd * FT, FT), bi)

    def scores(i, s_ref, x_ref):
        _, qd, kd, bi = item(i)
        s = lax.dot_general(qb[pl.ds(qd, FT), :], kb[pl.ds(kd, FT), :],
                            (((1,), (1,)), ((), ())), preferred_element_type=jnp.float32)
        s_ref[...] = s
        t = s[:, :HD]
        for l in range(HD, FT, HD):
            t = jnp.maximum(t, s[:, l:l + HD])
        top = jnp.broadcast_to(jnp.max(t, axis=1, keepdims=True), (FT, HD))
        x_ref[...] = top + bt[bi][0:1]

    def mix(i, s_ref, x_ref):
        qs, _, kd, bi = item(i)
        rows = pl.ds(qs, FT)
        old = mm[rows, :]
        new = jnp.maximum(old, x_ref[...])
        keep = jnp.exp2((old - new) * C)
        mm[rows, :] = new
        sub = new - bt[bi][0:1]
        w = [jnp.exp2((s_ref[:, l:l + HD] - sub) * C).astype(jnp.bfloat16)
             for l in range(0, FT, HD)]
        d = jnp.dot(jnp.concatenate(w, axis=1), vb[pl.ds(kd, FT), :],
                    preferred_element_type=jnp.float32)
        acc[rows, :HD] = acc[rows, :HD] * keep + d[:, :HD]
        acc[rows, HD:] = acc[rows, HD:] * keep + d[:, HD:]

    eye = (lax.broadcasted_iota(jnp.int32, (HD, HD), 0)
           == lax.broadcasted_iota(jnp.int32, (HD, HD), 1))

    def give_back(s):
        def body(b, carry):
            r = pl.multiple_of((2 + s) * FT + b * HD, HD)
            o = pl.multiple_of(s * FT + b * HD, HD)
            den = acc[pl.ds(r, HD), HD:]
            ro[pl.ds(o, HD), :] = (acc[pl.ds(r, HD), :HD] / den).astype(jnp.bfloat16)
            lse = mm[pl.ds(r, HD), :] + jnp.log2(den) * (1.0 / C)
            rs[s * 6 + b] = jnp.broadcast_to(
                jnp.sum(jnp.where(eye, lse, 0.0), axis=0, keepdims=True), (8, HD))
            return carry

        lax.fori_loop(0, 6, body, 0)

    def returns(s):
        return (rc(ro.at[pl.ds(s * FT, FT)], reto.at[pl.ds(s * FT, FT)], RO + s, RO + s, tm + 2, hd),
                rc(rs.at[pl.ds(s * 6, 6)], rets.at[pl.ds(s * 6, 6)], RT + s, RT + s, tm + 2, hd))

    relay = (rc(kf(4), kf(4), TK, TK, other, hd), rc(vf(4), vf(4), TV, TV, other, hd))

    def before(i):
        @pl.when(i == 3)
        def _():
            @pl.when(zh == 0)
            def _():
                def f(piece, full):
                    @pl.when(jnp.logical_not(root))
                    def _():
                        got(piece(x), SP + x)

                    for cp in stage2(piece):
                        cp.start()

                by_core(f)

        @pl.when(i == 4)
        def _():
            @pl.when(both(is0, has_prev))
            def _():
                send_q[0].wait_send()
                send_q[2].start()

            got(kf(2), PK0)
            got(vf(2), PV0)

            @pl.when(both(is0, has_next))
            def _():
                got(qb.at[pl.ds(2 * FT, FT)], RQ0)
                got(bt.at[pl.ds(12, 4)], RB)

        @pl.when(i == 6)
        def _():
            @pl.when(both(is0, has_next))
            def _():
                give_back(0)
                for cp in returns(0):
                    cp.start()

            def f(piece, full):
                @pl.when(zh > 0)
                def _():
                    got(piece(x), SP + x)

                for cp in stage3(piece):
                    cp.start()

            by_core(f)

            @pl.when(both(is0, has_prev))
            def _():
                got(kf(4), TK)
                got(vf(4), TV)
                for cp in relay:
                    cp.start()

            @pl.when(is1)
            def _():
                got(kf(3), PK1)
                got(vf(3), PV1)

        @pl.when(i == 8)
        def _():
            @pl.when(both(is0, has_next))
            def _():
                got(qb.at[pl.ds(3 * FT, FT)], RQ1)

            @pl.when(both(is1, has_prev))
            def _():
                got(kf(4), TK)
                got(vf(4), TV)

        @pl.when(i == 9)
        def _():
            @pl.when(both(is0, has_next))
            def _():
                give_back(1)
                for cp in returns(1):
                    cp.start()

            def f(piece, full):
                for p in range(4):
                    @pl.when(x != p)
                    def _():
                        got(piece(p), SP + p)

                stage4(full).start()

            by_core(f)

            @pl.when(is0)
            def _():
                got(vf(5), SF)

            @pl.when(is1)
            def _():
                got(kf(5), SF)

    def step(i, carry):
        before(i)
        scores(i, s0, x0)
        mix(i, s0, x0)
        return carry

    lax.fori_loop(0, 11, step, 0)

    def finish(s):
        merged = both(is0, has_prev)

        @pl.when(merged)
        def _():
            got(reto.at[pl.ds(s * FT, FT)], RO + s)
            got(rets.at[pl.ds(s * 6, 6)], RT + s)

            def body(b, carry):
                r = pl.multiple_of(s * FT + b * HD, HD)
                row = jnp.broadcast_to(rets[s * 6 + b][0:1], (HD, HD))
                far = jnp.broadcast_to(
                    jnp.sum(jnp.where(eye, row, 0.0), axis=1, keepdims=True), (HD, HD))
                old = mm[pl.ds(r, HD), :]
                new = jnp.maximum(old, far)
                a = jnp.exp2((old - new) * C)
                b2 = jnp.exp2((far - new) * C)
                num = acc[pl.ds(r, HD), :HD] * a + reto[pl.ds(r, HD), :].astype(jnp.float32) * b2
                den = acc[pl.ds(r, HD), HD:] * a + b2
                att[pl.ds(r, HD), :] = (num / den).astype(jnp.bfloat16)
                return carry

            lax.fori_loop(0, 6, body, 0)

        @pl.when(jnp.logical_not(merged))
        def _():
            def body(b, carry):
                r = pl.multiple_of(s * FT + b * HD, HD)
                att[pl.ds(r, HD), :] = (acc[pl.ds(r, HD), :HD] / acc[pl.ds(r, HD), HD:]).astype(jnp.bfloat16)
                return carry

            lax.fori_loop(0, 6, body, 0)

    def block(j):
        return rc(att.at[pl.ds(j * BLK, BLK)], gath.at[hd], SH + j, RH + hd, tm, j)

    for s in range(2):
        finish(s)
        for j in range(4 * s, 4 * s + 4):
            @pl.when(j != hd)
            def _():
                block(j).start()

            @pl.when(j == hd)
            def _():
                gath[hd] = att[pl.ds(j * BLK, BLK), :]

    for e in range(8):
        @pl.when(e != hd)
        def _():
            got(gath.at[e], RH + e)
        out_ref[:, e * HD:(e + 1) * HD] = gath[e]

    for cp in par[:2]:
        cp.wait_send()

    @pl.when(is0)
    def _():
        for cp in par[2:]:
            cp.wait_send()

    def drain(piece, full):
        for cp in stage3(piece):
            cp.wait_send()
        stage4(full).wait_send()

        @pl.when(zh == 0)
        def _():
            for cp in stage2(piece):
                cp.wait_send()

    by_core(drain)

    @pl.when(both(is0, has_prev))
    def _():
        for cp in send_q[1:]:
            cp.wait_send()
        for cp in relay:
            cp.wait_send()

    @pl.when(both(is0, has_next))
    def _():
        for s in range(2):
            for cp in returns(s):
                cp.wait_send()

    @pl.when(both(is1, has_next))
    def _():
        for cp in send_t:
            cp.wait_send()

    @pl.when(root)
    def _():
        for cp in stage1:
            cp.wait_send()

    for j in range(8):
        @pl.when(j != hd)
        def _():
            block(j).wait_send()


def local(query_states, key_states, value_states, win_start, group_end, out_weight):
    rows = pl.pallas_call(
        kernel,
        out_shape=jax.ShapeDtypeStruct((BLK, 8 * HD), jnp.bfloat16),
        in_specs=[pl.BlockSpec(memory_space=pltpu.HBM)] * 5,
        out_specs=pl.BlockSpec(memory_space=pltpu.VMEM),
        scratch_shapes=[
            pltpu.SMEM((2,), jnp.int32),
            pltpu.SMEM((2,), jnp.int32),
            pltpu.VMEM((4 * FT, HD), jnp.bfloat16),
            pltpu.VMEM((6 * FT, HD), jnp.bfloat16),
            pltpu.VMEM((6 * FT, 2 * HD), jnp.bfloat16),
            pltpu.VMEM((4 * FT, 2 * HD), jnp.float32),
            pltpu.VMEM((4 * FT, HD), jnp.float32),
            pltpu.VMEM((FT, FT), jnp.float32),
            pltpu.VMEM((FT, HD), jnp.float32),
            pltpu.VMEM((16, 8, HD), jnp.float32),
            pltpu.VMEM((4, 8, HD), jnp.float32),
            pltpu.VMEM((2 * FT, HD), jnp.bfloat16),
            pltpu.VMEM((2 * FT, HD), jnp.bfloat16),
            pltpu.VMEM((12, 8, HD), jnp.float32),
            pltpu.VMEM((2 * FT, HD), jnp.bfloat16),
            pltpu.VMEM((12, 8, HD), jnp.float32),
            pltpu.VMEM((8, BLK, HD), jnp.bfloat16),
            pltpu.SemaphoreType.DMA((6,)),
            pltpu.SemaphoreType.DMA((35,)),
            pltpu.SemaphoreType.DMA((26,)),
        ],
        compiler_params=pltpu.CompilerParams(
            collective_id=0, has_side_effects=True, vmem_limit_bytes=63000000),
        name="attend",
    )(query_states, key_states, value_states, win_start, group_end)
    return jnp.dot(rows, out_weight, preferred_element_type=jnp.float32).astype(jnp.bfloat16)


def solution(mesh):
    in_specs = (P("tm", "head"), P("tm", "head"), P("tm", "head"), P("tm"), P("tm"), P())
    out_specs = P(("tm", "head"), None)
    return jax.shard_map(local, mesh=mesh, in_specs=in_specs, out_specs=out_specs, check_vma=False)
```

```python
import jax
import jax.numpy as jnp
from jax import lax
from jax.experimental import pallas as pl
from jax.experimental.pallas import tpu as pltpu
from jax.sharding import PartitionSpec as P

HD = 128
FT = 768
BLK = 192
C = HD**-0.5 * 1.4426950408889634
HIDE = -1.0e6
LOW = -3.0e6
MESH = pl.DeviceIdType.MESH

Q0 = (0, 1, 2, 2, 0, 3, 1, 0, 1, 0, 1)
K0 = (0, 0, 1, 2, 1, 2, 1, 4, 4, 5, 5)
Q1 = (0, 1, 0, 1, 0, 1, 0, 1, 1, 0, 0)
K1 = (0, 0, 1, 1, 2, 2, 3, 3, 5, 5, 4)

PK0, PV0, PK1, PV1, TK, TV, RQ0, RQ1, RB, RO, RT, SK, SV, RH = (
    0, 1, 2, 3, 4, 5, 6, 7, 8, 9, 11, 13, 17, 21)
S1S, S2S, S3S, S4S, SH = 13, 21, 27, 33, 41


def kernel(q_hbm, k_hbm, v_hbm, ws_hbm, ge_hbm, out_ref, ws, ge, qb, kb, vb, acc, mm, s0, s1, x0, x1,
           bt, bs, att, ro, rs, reto, rets, gath, lsem, ssem, rsem):
    tm = lax.axis_index("tm")
    hd = lax.axis_index("head")
    core = lax.rem(tm, 2)
    c = lax.div(tm, 2)
    x = lax.div(c, 4)
    zh = lax.rem(c, 4)
    other = tm + 1 - 2 * core
    has_prev = c > 0
    has_next = c < 15
    first = (c == 0).astype(jnp.int32)
    last = (c == 15).astype(jnp.int32)
    is0 = core == 0
    is1 = core == 1

    def both(*conds):
        r = conds[0]
        for d in conds[1:]:
            r = jnp.logical_and(r, d)
        return r

    def rc(src, dst, si, ri, t, h):
        return pltpu.make_async_remote_copy(
            src_ref=src, dst_ref=dst, send_sem=ssem.at[si], recv_sem=rsem.at[ri],
            device_id=(t, h), device_id_type=MESH)

    def got(dst, ri):
        rc(dst, dst, 0, ri, other, hd).wait_recv()

    def sent(src, si):
        rc(src, src, si, 0, other, hd).wait_send()

    def kf(n):
        return kb.at[pl.ds(n * FT, FT)]

    def vf(n):
        return vb.at[pl.ds(n * FT, FT), pl.ds(0, HD)]

    def kp(p):
        return kb.at[pl.ds(pl.multiple_of(5 * FT + p * BLK, BLK), BLK)]

    def vp(p):
        return vb.at[pl.ds(pl.multiple_of(5 * FT + p * BLK, BLK), BLK), pl.ds(0, HD)]

    barrier = pltpu.get_barrier_semaphore()

    def hello(t, h):
        pl.semaphore_signal(barrier, inc=1, device_id=(t, h), device_id_type=MESH)

    own = (
        pltpu.make_async_copy(q_hbm, qb.at[pl.ds(0, 2 * FT)], lsem.at[0]),
        pltpu.make_async_copy(k_hbm, kb.at[pl.ds(0, 2 * FT)], lsem.at[1]),
        pltpu.make_async_copy(v_hbm, vb.at[pl.ds(0, 2 * FT), pl.ds(0, HD)], lsem.at[2]),
    )
    for cp in own:
        cp.start()
    limits = (pltpu.make_async_copy(ws_hbm, ws, lsem.at[4]), pltpu.make_async_copy(ge_hbm, ge, lsem.at[5]))
    for cp in limits:
        cp.start()

    vb[:, HD:] = jnp.ones((6 * FT, HD), jnp.bfloat16)

    hello(other, hd)
    for d in range(1, 8):
        hello(tm, lax.rem(hd + d, 8))
    @pl.when(is1)
    def _():
        for d in range(1, 4):
            hello(2 * (lax.rem(x + d, 4) * 4 + zh) + 1, hd)

    @pl.when(both(is0, has_prev))
    def _():
        hello(tm - 2, hd)
        hello(tm - 1, hd)

    @pl.when(both(is0, has_next))
    def _():
        hello(tm + 2, hd)

    @pl.when(both(is1, lax.rem(zh, 2) == 1))
    def _():
        hello(8 * x + 1, hd)

    @pl.when(both(is1, zh == 2))
    def _():
        hello(tm + 2, hd)

    @pl.when(both(is1, zh == 0, x > 0))
    def _():
        hello(0, hd)

    root = both(is0, c == 0)

    def bias(slot, frame):
        seen = jnp.logical_and(frame >= 1, jnp.logical_and(frame >= ws[slot], frame <= ge[slot]))
        return jnp.full((8, HD), jnp.where(seen, 0.0, HIDE), jnp.float32)

    for cp in limits:
        cp.wait()
    base = 2 * tm
    part = 2 * other
    for s in range(2):
        bt[s * 6 + 0] = bias(s, base)
        bt[s * 6 + 1] = bias(s, base + 1)
        bt[s * 6 + 2] = bias(s, part)
        bt[s * 6 + 3] = bias(s, part + 1)
        bt[s * 6 + 4] = bias(s, 4 * c - 1)
        bt[s * 6 + 5] = jnp.zeros((8, HD), jnp.float32)
    for s in range(2):
        for m in range(2):
            bs[2 * s + m] = bias(s, 4 * c - 3 + m)

    low = (zh == 0).astype(jnp.int32)
    pl.semaphore_wait(barrier, 8 + (1 - core) * (2 - last - first + 3 * first) + core * (3 + 2 * low + lax.div(zh, 3) + 1 - last))

    par = [
        rc(k_hbm.at[pl.ds(0, FT)], kf(2), PK0, PK0, other, hd),
        rc(v_hbm.at[pl.ds(0, FT)], vf(2), PV0, PV0, other, hd),
        rc(k_hbm.at[pl.ds(FT, FT)], kf(3), PK1, PK1, other, hd),
        rc(v_hbm.at[pl.ds(FT, FT)], vf(3), PV1, PV1, other, hd),
    ]
    send_q = [
        rc(q_hbm.at[pl.ds(0, FT)], qb.at[pl.ds(2 * FT, FT)], RQ0, RQ0, tm - 2, hd),
        rc(bs, bt.at[pl.ds(12, 4)], RB, RB, tm - 2, hd),
        rc(q_hbm.at[pl.ds(FT, FT)], qb.at[pl.ds(3 * FT, FT)], RQ1, RQ1, tm - 2, hd),
    ]
    send_t = [
        rc(k_hbm.at[pl.ds(FT, FT)], kf(4), TK, TK, tm + 1, hd),
        rc(v_hbm.at[pl.ds(FT, FT)], vf(4), TV, TV, tm + 1, hd),
    ]

    @pl.when(both(is0, has_prev))
    def _():
        send_q[0].start()
        send_q[1].start()

    @pl.when(both(is1, has_next))
    def _():
        send_t[0].start()

    @pl.when(both(is1, has_next, zh > 0))
    def _():
        send_t[1].start()

    stage1 = []
    for d in range(4):
        rows = pl.ds(d * BLK, BLK)
        stage1.append(rc(k_hbm.at[rows], kp(d), S1S + 2 * d, SK + d, 8 * d + 1, hd))
        stage1.append(rc(v_hbm.at[rows], vp(d), S1S + 2 * d + 1, SV + d, 8 * d + 1, hd))

    @pl.when(root)
    def _():
        for cp in stage1:
            cp.start()

    stage2 = []
    for d in (1, 3):
        t = 2 * (x * 4 + d) + 1
        stage2.append(rc(kp(x), kp(x), S2S + d - 1, SK + x, t, hd))
        stage2.append(rc(vp(x), vp(x), S2S + d, SV + x, t, hd))
    stage2b = (rc(kp(x), kp(x), S2S, SK + x, tm - 2, hd), rc(vp(x), vp(x), S2S + 1, SV + x, tm - 2, hd))
    stage3 = []
    for d in (2, 1, 3):
        t = 2 * (lax.rem(x + d, 4) * 4 + zh) + 1
        stage3.append(rc(kp(x), kp(x), S3S + 2 * d - 2, SK + x, t, hd))
        stage3.append(rc(vp(x), vp(x), S3S + 2 * d - 1, SV + x, t, hd))

    def stage4(p):
        return (rc(kp(p), kp(p), S4S + 2 * p, SK + p, other, hd), rc(vp(p), vp(p), S4S + 2 * p + 1, SV + p, other, hd))

    mm[...] = jnp.full_like(mm, LOW)
    acc[...] = jnp.zeros_like(acc)

    for cp in own:
        cp.wait()

    def pick(i, a, b):
        r = a[0] + core * (b[0] - a[0])
        for m in range(1, len(a)):
            r = jnp.where(i == m, a[m] + core * (b[m] - a[m]), r)
        return r

    def item(i):
        qs = pick(i, Q0, Q1)
        ks = pick(i, K0, K1)
        qd = qs - 2 * last * lax.div(qs, 2)
        kd = ks - 4 * first * (lax.div(ks, 4) - lax.div(ks, 5))
        far = lax.div(qs, 2)
        bi = (1 - far) * (qs * 6 + ks) + far * (12 + (qs - 2) * 2 + ks - 1)
        return (pl.multiple_of(qs * FT, FT), pl.multiple_of(qd * FT, FT),
                pl.multiple_of(kd * FT, FT), bi)

    def scores(i, s_ref, x_ref):
        _, qd, kd, bi = item(i)
        s = lax.dot_general(qb[pl.ds(qd, FT), :], kb[pl.ds(kd, FT), :],
                            (((1,), (1,)), ((), ())), preferred_element_type=jnp.float32)
        s_ref[...] = s
        t = s[:, :HD]
        for l in range(HD, FT, HD):
            t = jnp.maximum(t, s[:, l:l + HD])
        top = jnp.broadcast_to(jnp.max(t, axis=1, keepdims=True), (FT, HD))
        x_ref[...] = top + bt[bi][0:1]

    def mix(i, s_ref, x_ref):
        qs, _, kd, bi = item(i)
        rows = pl.ds(qs, FT)
        old = mm[rows, :]
        new = jnp.maximum(old, x_ref[...])
        keep = jnp.exp2((old - new) * C)
        mm[rows, :] = new
        sub = new - bt[bi][0:1]
        w = [jnp.exp2((s_ref[:, l:l + HD] - sub) * C).astype(jnp.bfloat16)
             for l in range(0, FT, HD)]
        d = jnp.dot(jnp.concatenate(w, axis=1), vb[pl.ds(kd, FT), :],
                    preferred_element_type=jnp.float32)
        acc[rows, :HD] = acc[rows, :HD] * keep + d[:, :HD]
        acc[rows, HD:] = acc[rows, HD:] * keep + d[:, HD:]

    eye = (lax.broadcasted_iota(jnp.int32, (HD, HD), 0)
           == lax.broadcasted_iota(jnp.int32, (HD, HD), 1))

    def give_back(s):
        def body(b, carry):
            r = pl.multiple_of((2 + s) * FT + b * HD, HD)
            o = pl.multiple_of(s * FT + b * HD, HD)
            den = acc[pl.ds(r, HD), HD:]
            ro[pl.ds(o, HD), :] = (acc[pl.ds(r, HD), :HD] / den).astype(jnp.bfloat16)
            lse = mm[pl.ds(r, HD), :] + jnp.log2(den) * (1.0 / C)
            rs[s * 6 + b] = jnp.broadcast_to(
                jnp.sum(jnp.where(eye, lse, 0.0), axis=0, keepdims=True), (8, HD))
            return carry

        lax.fori_loop(0, 6, body, 0)

    def returns(s):
        return (rc(ro.at[pl.ds(s * FT, FT)], reto.at[pl.ds(s * FT, FT)], RO + s, RO + s, tm + 2, hd),
                rc(rs.at[pl.ds(s * 6, 6)], rets.at[pl.ds(s * 6, 6)], RT + s, RT + s, tm + 2, hd))

    relay = (rc(kf(4), kf(4), TK, TK, other, hd), rc(vf(4), vf(4), TV, TV, other, hd))

    def finish(s):
        merged = both(is0, has_prev)

        @pl.when(merged)
        def _():
            got(reto.at[pl.ds(s * FT, FT)], RO + s)
            got(rets.at[pl.ds(s * 6, 6)], RT + s)

            def body(b, carry):
                r = pl.multiple_of(s * FT + b * HD, HD)
                row = jnp.broadcast_to(rets[s * 6 + b][0:1], (HD, HD))
                far = jnp.broadcast_to(
                    jnp.sum(jnp.where(eye, row, 0.0), axis=1, keepdims=True), (HD, HD))
                old = mm[pl.ds(r, HD), :]
                new = jnp.maximum(old, far)
                a = jnp.exp2((old - new) * C)
                b2 = jnp.exp2((far - new) * C)
                num = acc[pl.ds(r, HD), :HD] * a + reto[pl.ds(r, HD), :].astype(jnp.float32) * b2
                den = acc[pl.ds(r, HD), HD:] * a + b2
                att[pl.ds(r, HD), :] = (num / den).astype(jnp.bfloat16)
                return carry

            lax.fori_loop(0, 6, body, 0)

        @pl.when(jnp.logical_not(merged))
        def _():
            def body(b, carry):
                r = pl.multiple_of(s * FT + b * HD, HD)
                att[pl.ds(r, HD), :] = (acc[pl.ds(r, HD), :HD] / acc[pl.ds(r, HD), HD:]).astype(jnp.bfloat16)
                return carry

            lax.fori_loop(0, 6, body, 0)

    def block(j):
        return rc(att.at[pl.ds(j * BLK, BLK)], gath.at[hd], SH + j, RH + hd, tm, j)

    def deliver(s):
        finish(s)
        for j in range(4 * s, 4 * s + 4):
            @pl.when(j != hd)
            def _():
                block(j).start()

            @pl.when(j == hd)
            def _():
                gath[hd] = att[pl.ds(j * BLK, BLK), :]

    def before(i):
        @pl.when(i == 1 + 2 * core)
        def _():
            for cp in par[:2]:
                cp.start()

        @pl.when(both(is1, zh == 0, i == 3))
        def _():
            got(kp(x), SK + x)
            got(vp(x), SV + x)
            for cp in stage2[:2]:
                cp.start()

            @pl.when(has_next)
            def _():
                send_t[1].start()

        @pl.when(both(is0, i == 2))
        def _():
            for cp in par[2:]:
                cp.start()

            @pl.when(has_prev)
            def _():
                send_q[0].wait_send()
                send_q[2].start()

            @pl.when(has_next)
            def _():
                got(qb.at[pl.ds(2 * FT, FT)], RQ0)
                got(bt.at[pl.ds(12, 4)], RB)

        @pl.when(i == 3 + core)
        def _():
            got(kf(2), PK0)
            got(vf(2), PV0)

        @pl.when(both(is0, has_next, i == 5))
        def _():
            give_back(0)
            for cp in returns(0):
                cp.start()
            got(qb.at[pl.ds(3 * FT, FT)], RQ1)

        @pl.when(both(is0, has_next, i == 7))
        def _():
            give_back(1)
            for cp in returns(1):
                cp.start()

        @pl.when(both(is1, zh == 0, i == 5))
        def _():
            for cp in stage2[2:]:
                cp.start()

        @pl.when(both(is1, i == 6))
        def _():
            got(kf(3), PK1)
            got(vf(3), PV1)

        @pl.when(both(is0, has_prev, i == 7))
        def _():
            got(kf(4), TK)
            got(vf(4), TV)
            for cp in relay:
                cp.start()

        @pl.when(both(is1, i == 8))
        def _():
            @pl.when(zh > 0)
            def _():
                got(kp(x), SK + x)
                got(vp(x), SV + x)

            @pl.when(zh == 3)
            def _():
                for cp in stage2b:
                    cp.start()

            for cp in stage3:
                cp.start()
            for d in range(4):
                p = lax.rem(x + d, 4)
                if d:
                    got(kp(p), SK + p)
                    got(vp(p), SV + p)
                for cp in stage4(p):
                    cp.start()

        @pl.when(both(is0, i == 9))
        def _():
            for p in range(4):
                got(kp(p), SK + p)
                got(vp(p), SV + p)

        @pl.when(both(is1, i == 10))
        def _():
            deliver(1)

            @pl.when(has_prev)
            def _():
                got(kf(4), TK)
                got(vf(4), TV)

    scores(0, s0, x0)

    def step(h, carry):
        i = 2 * h
        before(i + 1)
        scores(i + 1, s1, x1)
        mix(i, s0, x0)
        before(i + 2)
        scores(i + 2, s0, x0)
        mix(i + 1, s1, x1)
        return carry

    lax.fori_loop(0, 5, step, 0)
    mix(10, s0, x0)

    deliver(0)

    @pl.when(is0)
    def _():
        deliver(1)

    for e in range(8):
        @pl.when(e != hd)
        def _():
            got(gath.at[e], RH + e)
        out_ref[:, e * HD:(e + 1) * HD] = gath[e]

    for cp in par[:2]:
        cp.wait_send()

    @pl.when(is0)
    def _():
        for cp in par[2:]:
            cp.wait_send()

    @pl.when(is1)
    def _():
        for cp in stage3:
            cp.wait_send()
        for p in range(4):
            for cp in stage4(p):
                cp.wait_send()

    @pl.when(both(is1, zh == 0))
    def _():
        for cp in stage2:
            cp.wait_send()

    @pl.when(both(is1, zh == 3))
    def _():
        for cp in stage2b:
            cp.wait_send()

    @pl.when(both(is0, has_prev))
    def _():
        for cp in send_q[1:]:
            cp.wait_send()
        for cp in relay:
            cp.wait_send()

    @pl.when(both(is0, has_next))
    def _():
        for s in range(2):
            for cp in returns(s):
                cp.wait_send()

    @pl.when(both(is1, has_next))
    def _():
        for cp in send_t:
            cp.wait_send()

    @pl.when(root)
    def _():
        for cp in stage1:
            cp.wait_send()

    for j in range(8):
        @pl.when(j != hd)
        def _():
            block(j).wait_send()


def local(query_states, key_states, value_states, win_start, group_end, out_weight):
    query_states, key_states, value_states, win_start, group_end = (
        pltpu.with_memory_space_constraint(a, pltpu.HBM)
        for a in (query_states, key_states, value_states, win_start, group_end))
    rows = pl.pallas_call(
        kernel,
        out_shape=jax.ShapeDtypeStruct((BLK, 8 * HD), jnp.bfloat16),
        in_specs=[pl.BlockSpec(memory_space=pltpu.HBM)] * 5,
        out_specs=pl.BlockSpec(memory_space=pltpu.VMEM),
        scratch_shapes=[
            pltpu.SMEM((2,), jnp.int32),
            pltpu.SMEM((2,), jnp.int32),
            pltpu.VMEM((4 * FT, HD), jnp.bfloat16),
            pltpu.VMEM((6 * FT, HD), jnp.bfloat16),
            pltpu.VMEM((6 * FT, 2 * HD), jnp.bfloat16),
            pltpu.VMEM((4 * FT, 2 * HD), jnp.float32),
            pltpu.VMEM((4 * FT, HD), jnp.float32),
            pltpu.VMEM((FT, FT), jnp.float32),
            pltpu.VMEM((FT, FT), jnp.float32),
            pltpu.VMEM((FT, HD), jnp.float32),
            pltpu.VMEM((FT, HD), jnp.float32),
            pltpu.VMEM((16, 8, HD), jnp.float32),
            pltpu.VMEM((4, 8, HD), jnp.float32),
            pltpu.VMEM((2 * FT, HD), jnp.bfloat16),
            pltpu.VMEM((2 * FT, HD), jnp.bfloat16),
            pltpu.VMEM((12, 8, HD), jnp.float32),
            pltpu.VMEM((2 * FT, HD), jnp.bfloat16),
            pltpu.VMEM((12, 8, HD), jnp.float32),
            pltpu.VMEM((8, BLK, HD), jnp.bfloat16),
            pltpu.SemaphoreType.DMA((6,)),
            pltpu.SemaphoreType.DMA((49,)),
            pltpu.SemaphoreType.DMA((29,)),
        ],
        compiler_params=pltpu.CompilerParams(
            collective_id=0, has_side_effects=True, vmem_limit_bytes=36000000),
        name="attend",
    )(query_states, key_states, value_states, win_start, group_end)
    return jnp.dot(rows, out_weight, preferred_element_type=jnp.float32).astype(jnp.bfloat16)


def solution(mesh):
    in_specs = (P("tm", "head"), P("tm", "head"), P("tm", "head"), P("tm"), P("tm"), P())
    out_specs = P(("tm", "head"), None)
    return jax.shard_map(local, mesh=mesh, in_specs=in_specs, out_specs=out_specs, check_vma=False)
```

```python
import jax
import jax.numpy as jnp
from jax import lax
from jax.experimental import pallas as pl
from jax.experimental.pallas import tpu as pltpu
from jax.sharding import PartitionSpec as P

HD = 128
FT = 768
BLK = 192
C = HD**-0.5 * 1.4426950408889634
HIDE = -1.0e6
LOW = -3.0e6
MESH = pl.DeviceIdType.MESH

Q0 = (0, 1, 2, 2, 0, 3, 1, 0, 1, 0, 1)
K0 = (0, 0, 1, 2, 1, 2, 1, 4, 4, 5, 5)
Q1 = (0, 1, 0, 1, 0, 1, 0, 1, 1, 0, 0)
K1 = (0, 0, 1, 1, 2, 2, 3, 3, 5, 5, 4)

PK0, PV0, PK1, PV1, TK, TV, RQ0, RQ1, RB, RO, RT, SK, SV, RH = (
    0, 1, 2, 3, 4, 5, 6, 7, 8, 9, 11, 13, 17, 21)
S1S, S2S, S3S, S4S, SH = 13, 21, 27, 33, 41


def kernel(q_hbm, k_hbm, v_hbm, ws_hbm, ge_hbm, out_ref, ws, ge, qb, kb, vb, acc, mm, s0, s1, x0, x1,
           bt, bs, att, ro, rs, reto, rets, gath, lsem, ssem, rsem):
    tm = lax.axis_index("tm")
    hd = lax.axis_index("head")
    core = lax.rem(tm, 2)
    c = lax.div(tm, 2)
    x = lax.div(c, 4)
    zh = lax.rem(c, 4)
    other = tm + 1 - 2 * core
    has_prev = c > 0
    has_next = c < 15
    first = (c == 0).astype(jnp.int32)
    last = (c == 15).astype(jnp.int32)
    is0 = core == 0
    is1 = core == 1

    def both(*conds):
        r = conds[0]
        for d in conds[1:]:
            r = jnp.logical_and(r, d)
        return r

    def rc(src, dst, si, ri, t, h):
        return pltpu.make_async_remote_copy(
            src_ref=src, dst_ref=dst, send_sem=ssem.at[si], recv_sem=rsem.at[ri],
            device_id=(t, h), device_id_type=MESH)

    def got(dst, ri):
        rc(dst, dst, 0, ri, other, hd).wait_recv()

    def sent(src, si):
        rc(src, src, si, 0, other, hd).wait_send()

    def kf(n):
        return kb.at[pl.ds(n * FT, FT)]

    def vf(n):
        return vb.at[pl.ds(n * FT, FT), pl.ds(0, HD)]

    def kp(p):
        return kb.at[pl.ds(pl.multiple_of(5 * FT + p * BLK, BLK), BLK)]

    def vp(p):
        return vb.at[pl.ds(pl.multiple_of(5 * FT + p * BLK, BLK), BLK), pl.ds(0, HD)]

    barrier = pltpu.get_barrier_semaphore()

    def hello(t, h):
        pl.semaphore_signal(barrier, inc=1, device_id=(t, h), device_id_type=MESH)

    own = (
        pltpu.make_async_copy(q_hbm, qb.at[pl.ds(0, 2 * FT)], lsem.at[0]),
        pltpu.make_async_copy(k_hbm, kb.at[pl.ds(0, 2 * FT)], lsem.at[1]),
        pltpu.make_async_copy(v_hbm, vb.at[pl.ds(0, 2 * FT), pl.ds(0, HD)], lsem.at[2]),
    )
    for cp in own:
        cp.start()
    limits = (pltpu.make_async_copy(ws_hbm, ws, lsem.at[4]), pltpu.make_async_copy(ge_hbm, ge, lsem.at[5]))
    for cp in limits:
        cp.start()

    vb[:, HD:] = jnp.ones((6 * FT, HD), jnp.bfloat16)

    hello(other, hd)
    for d in range(1, 8):
        hello(tm, lax.rem(hd + d, 8))
    @pl.when(is1)
    def _():
        for d in range(1, 4):
            hello(2 * (lax.rem(x + d, 4) * 4 + zh) + 1, hd)

    @pl.when(both(is0, has_prev))
    def _():
        hello(tm - 2, hd)
        hello(tm - 1, hd)

    @pl.when(both(is0, has_next))
    def _():
        hello(tm + 2, hd)

    @pl.when(both(is1, zh > 0))
    def _():
        hello(tm - 2 - 4 * lax.div(zh, 3), hd)

    @pl.when(both(is1, zh == 0, x > 0))
    def _():
        hello(0, hd)

    root = both(is0, c == 0)

    def bias(slot, frame):
        seen = jnp.logical_and(frame >= 1, jnp.logical_and(frame >= ws[slot], frame <= ge[slot]))
        return jnp.full((8, HD), jnp.where(seen, 0.0, HIDE), jnp.float32)

    for cp in limits:
        cp.wait()
    base = 2 * tm
    part = 2 * other
    for s in range(2):
        bt[s * 6 + 0] = bias(s, base)
        bt[s * 6 + 1] = bias(s, base + 1)
        bt[s * 6 + 2] = bias(s, part)
        bt[s * 6 + 3] = bias(s, part + 1)
        bt[s * 6 + 4] = bias(s, 4 * c - 1)
        bt[s * 6 + 5] = jnp.zeros((8, HD), jnp.float32)
    for s in range(2):
        for m in range(2):
            bs[2 * s + m] = bias(s, 4 * c - 3 + m)

    low = 2 - zh + lax.div(zh, 3)
    pl.semaphore_wait(barrier, 8 + (1 - core) * (2 - last - first + 3 * first) + core * (3 + low + 1 - last))

    par = [
        rc(k_hbm.at[pl.ds(0, FT)], kf(2), PK0, PK0, other, hd),
        rc(v_hbm.at[pl.ds(0, FT)], vf(2), PV0, PV0, other, hd),
        rc(k_hbm.at[pl.ds(FT, FT)], kf(3), PK1, PK1, other, hd),
        rc(v_hbm.at[pl.ds(FT, FT)], vf(3), PV1, PV1, other, hd),
    ]
    send_q = [
        rc(q_hbm.at[pl.ds(0, FT)], qb.at[pl.ds(2 * FT, FT)], RQ0, RQ0, tm - 2, hd),
        rc(bs, bt.at[pl.ds(12, 4)], RB, RB, tm - 2, hd),
        rc(q_hbm.at[pl.ds(FT, FT)], qb.at[pl.ds(3 * FT, FT)], RQ1, RQ1, tm - 2, hd),
    ]
    send_t = [
        rc(k_hbm.at[pl.ds(FT, FT)], kf(4), TK, TK, tm + 1, hd),
        rc(v_hbm.at[pl.ds(FT, FT)], vf(4), TV, TV, tm + 1, hd),
    ]

    @pl.when(both(is0, has_prev))
    def _():
        send_q[0].start()
        send_q[1].start()

    @pl.when(both(is1, has_next))
    def _():
        send_t[0].start()

    @pl.when(both(is1, has_next, zh > 0))
    def _():
        send_t[1].start()

    stage1 = []
    for d in range(4):
        rows = pl.ds(d * BLK, BLK)
        stage1.append(rc(k_hbm.at[rows], kp(d), S1S + 2 * d, SK + d, 8 * d + 1, hd))
        stage1.append(rc(v_hbm.at[rows], vp(d), S1S + 2 * d + 1, SV + d, 8 * d + 1, hd))

    @pl.when(root)
    def _():
        for cp in stage1:
            cp.start()

    stage2 = (rc(kp(x), kp(x), S2S, SK + x, tm + 2, hd), rc(vp(x), vp(x), S2S + 1, SV + x, tm + 2, hd))
    stage2b = (rc(kp(x), kp(x), S2S + 2, SK + x, tm + 6, hd), rc(vp(x), vp(x), S2S + 3, SV + x, tm + 6, hd))
    stage3 = []
    for d in (2, 1, 3):
        t = 2 * (lax.rem(x + d, 4) * 4 + zh) + 1
        stage3.append(rc(kp(x), kp(x), S3S + 2 * d - 2, SK + x, t, hd))
        stage3.append(rc(vp(x), vp(x), S3S + 2 * d - 1, SV + x, t, hd))

    def stage4(p):
        return (rc(kp(p), kp(p), S4S + 2 * p, SK + p, other, hd), rc(vp(p), vp(p), S4S + 2 * p + 1, SV + p, other, hd))

    mm[...] = jnp.full_like(mm, LOW)
    acc[...] = jnp.zeros_like(acc)

    for cp in own:
        cp.wait()

    def pick(i, a, b):
        r = a[0] + core * (b[0] - a[0])
        for m in range(1, len(a)):
            r = jnp.where(i == m, a[m] + core * (b[m] - a[m]), r)
        return r

    def item(i):
        qs = pick(i, Q0, Q1)
        ks = pick(i, K0, K1)
        qd = qs - 2 * last * lax.div(qs, 2)
        kd = ks - 4 * first * (lax.div(ks, 4) - lax.div(ks, 5))
        far = lax.div(qs, 2)
        bi = (1 - far) * (qs * 6 + ks) + far * (12 + (qs - 2) * 2 + ks - 1)
        return (pl.multiple_of(qs * FT, FT), pl.multiple_of(qd * FT, FT),
                pl.multiple_of(kd * FT, FT), bi)

    def scores(i, s_ref, x_ref):
        _, qd, kd, bi = item(i)
        s = lax.dot_general(qb[pl.ds(qd, FT), :], kb[pl.ds(kd, FT), :],
                            (((1,), (1,)), ((), ())), preferred_element_type=jnp.float32)
        s_ref[...] = s
        t = s[:, :HD]
        for l in range(HD, FT, HD):
            t = jnp.maximum(t, s[:, l:l + HD])
        top = jnp.broadcast_to(jnp.max(t, axis=1, keepdims=True), (FT, HD))
        x_ref[...] = top + bt[bi][0:1]

    def mix(i, s_ref, x_ref):
        qs, _, kd, bi = item(i)
        rows = pl.ds(qs, FT)
        old = mm[rows, :]
        new = jnp.maximum(old, x_ref[...])
        keep = jnp.exp2((old - new) * C)
        mm[rows, :] = new
        sub = new - bt[bi][0:1]
        w = [jnp.exp2((s_ref[:, l:l + HD] - sub) * C).astype(jnp.bfloat16)
             for l in range(0, FT, HD)]
        d = jnp.dot(jnp.concatenate(w, axis=1), vb[pl.ds(kd, FT), :],
                    preferred_element_type=jnp.float32)
        acc[rows, :HD] = acc[rows, :HD] * keep + d[:, :HD]
        acc[rows, HD:] = acc[rows, HD:] * keep + d[:, HD:]

    eye = (lax.broadcasted_iota(jnp.int32, (HD, HD), 0)
           == lax.broadcasted_iota(jnp.int32, (HD, HD), 1))

    def give_back(s):
        def body(b, carry):
            r = pl.multiple_of((2 + s) * FT + b * HD, HD)
            o = pl.multiple_of(s * FT + b * HD, HD)
            den = acc[pl.ds(r, HD), HD:]
            ro[pl.ds(o, HD), :] = (acc[pl.ds(r, HD), :HD] / den).astype(jnp.bfloat16)
            lse = mm[pl.ds(r, HD), :] + jnp.log2(den) * (1.0 / C)
            rs[s * 6 + b] = jnp.broadcast_to(
                jnp.sum(jnp.where(eye, lse, 0.0), axis=0, keepdims=True), (8, HD))
            return carry

        lax.fori_loop(0, 6, body, 0)

    def returns(s):
        return (rc(ro.at[pl.ds(s * FT, FT)], reto.at[pl.ds(s * FT, FT)], RO + s, RO + s, tm + 2, hd),
                rc(rs.at[pl.ds(s * 6, 6)], rets.at[pl.ds(s * 6, 6)], RT + s, RT + s, tm + 2, hd))

    relay = (rc(kf(4), kf(4), TK, TK, other, hd), rc(vf(4), vf(4), TV, TV, other, hd))

    def finish(s):
        merged = both(is0, has_prev)

        @pl.when(merged)
        def _():
            got(reto.at[pl.ds(s * FT, FT)], RO + s)
            got(rets.at[pl.ds(s * 6, 6)], RT + s)

            def body(b, carry):
                r = pl.multiple_of(s * FT + b * HD, HD)
                row = jnp.broadcast_to(rets[s * 6 + b][0:1], (HD, HD))
                far = jnp.broadcast_to(
                    jnp.sum(jnp.where(eye, row, 0.0), axis=1, keepdims=True), (HD, HD))
                old = mm[pl.ds(r, HD), :]
                new = jnp.maximum(old, far)
                a = jnp.exp2((old - new) * C)
                b2 = jnp.exp2((far - new) * C)
                num = acc[pl.ds(r, HD), :HD] * a + reto[pl.ds(r, HD), :].astype(jnp.float32) * b2
                den = acc[pl.ds(r, HD), HD:] * a + b2
                att[pl.ds(r, HD), :] = (num / den).astype(jnp.bfloat16)
                return carry

            lax.fori_loop(0, 6, body, 0)

        @pl.when(jnp.logical_not(merged))
        def _():
            def body(b, carry):
                r = pl.multiple_of(s * FT + b * HD, HD)
                att[pl.ds(r, HD), :] = (acc[pl.ds(r, HD), :HD] / acc[pl.ds(r, HD), HD:]).astype(jnp.bfloat16)
                return carry

            lax.fori_loop(0, 6, body, 0)

    def block(j):
        return rc(att.at[pl.ds(j * BLK, BLK)], gath.at[hd], SH + j, RH + hd, tm, j)

    def deliver(s):
        finish(s)
        for j in range(4 * s, 4 * s + 4):
            @pl.when(j != hd)
            def _():
                block(j).start()

            @pl.when(j == hd)
            def _():
                gath[hd] = att[pl.ds(j * BLK, BLK), :]

    def before(i):
        @pl.when(both(is0, has_prev, i == 1))
        def _():
            send_q[2].start()

        @pl.when(i == 1 + 2 * core)
        def _():
            for cp in par[:2]:
                cp.start()

        @pl.when(both(is1, zh == 0, i == 3))
        def _():
            got(kp(x), SK + x)
            got(vp(x), SV + x)
            for cp in stage2:
                cp.start()

            @pl.when(has_next)
            def _():
                send_t[1].start()

        @pl.when(both(is0, i == 2))
        def _():
            for cp in par[2:]:
                cp.start()

            @pl.when(has_next)
            def _():
                got(qb.at[pl.ds(2 * FT, FT)], RQ0)
                got(bt.at[pl.ds(12, 4)], RB)

        @pl.when(i == 3 + core)
        def _():
            got(kf(2), PK0)
            got(vf(2), PV0)

        @pl.when(both(is0, has_next, i == 5))
        def _():
            give_back(0)
            for cp in returns(0):
                cp.start()
            got(qb.at[pl.ds(3 * FT, FT)], RQ1)

        @pl.when(both(is0, has_next, i == 7))
        def _():
            give_back(1)
            for cp in returns(1):
                cp.start()

        @pl.when(both(is1, i == 6))
        def _():
            got(kf(3), PK1)
            got(vf(3), PV1)

        @pl.when(both(is0, has_prev, i == 7))
        def _():
            got(kf(4), TK)
            got(vf(4), TV)
            for cp in relay:
                cp.start()

        @pl.when(both(is1, i == 8))
        def _():
            @pl.when(zh > 0)
            def _():
                got(kp(x), SK + x)
                got(vp(x), SV + x)

            @pl.when(zh == 1)
            def _():
                for cp in stage2:
                    cp.start()

            for cp in stage3:
                cp.start()

            @pl.when(zh == 0)
            def _():
                for cp in stage2b:
                    cp.start()

            for d in range(4):
                p = lax.rem(x + d, 4)
                if d:
                    got(kp(p), SK + p)
                    got(vp(p), SV + p)
                for cp in stage4(p):
                    cp.start()

        @pl.when(both(is0, i == 9))
        def _():
            for p in range(4):
                got(kp(p), SK + p)
                got(vp(p), SV + p)

        @pl.when(both(is1, has_prev, i == 10))
        def _():
            got(kf(4), TK)
            got(vf(4), TV)

    scores(0, s0, x0)

    def step(h, carry):
        i = 2 * h
        before(i + 1)
        scores(i + 1, s1, x1)
        mix(i, s0, x0)
        before(i + 2)
        scores(i + 2, s0, x0)
        mix(i + 1, s1, x1)
        return carry

    lax.fori_loop(0, 5, step, 0)
    mix(10, s0, x0)

    deliver(0)
    deliver(1)

    for e in range(8):
        @pl.when(e != hd)
        def _():
            got(gath.at[e], RH + e)
        out_ref[:, e * HD:(e + 1) * HD] = gath[e]

    for cp in par[:2]:
        cp.wait_send()

    @pl.when(is0)
    def _():
        for cp in par[2:]:
            cp.wait_send()

    @pl.when(is1)
    def _():
        for cp in stage3:
            cp.wait_send()
        for p in range(4):
            for cp in stage4(p):
                cp.wait_send()

    @pl.when(both(is1, zh < 2))
    def _():
        for cp in stage2:
            cp.wait_send()

    @pl.when(both(is1, zh == 0))
    def _():
        for cp in stage2b:
            cp.wait_send()

    @pl.when(both(is0, has_prev))
    def _():
        for cp in send_q:
            cp.wait_send()
        for cp in relay:
            cp.wait_send()

    @pl.when(both(is0, has_next))
    def _():
        for s in range(2):
            for cp in returns(s):
                cp.wait_send()

    @pl.when(both(is1, has_next))
    def _():
        for cp in send_t:
            cp.wait_send()

    @pl.when(root)
    def _():
        for cp in stage1:
            cp.wait_send()

    for j in range(8):
        @pl.when(j != hd)
        def _():
            block(j).wait_send()


def local(query_states, key_states, value_states, win_start, group_end, out_weight):
    query_states, key_states, value_states, win_start, group_end = (
        pltpu.with_memory_space_constraint(a, pltpu.HBM)
        for a in (query_states, key_states, value_states, win_start, group_end))
    rows = pl.pallas_call(
        kernel,
        out_shape=jax.ShapeDtypeStruct((BLK, 8 * HD), jnp.bfloat16),
        in_specs=[pl.BlockSpec(memory_space=pltpu.HBM)] * 5,
        out_specs=pl.BlockSpec(memory_space=pltpu.VMEM),
        scratch_shapes=[
            pltpu.SMEM((2,), jnp.int32),
            pltpu.SMEM((2,), jnp.int32),
            pltpu.VMEM((4 * FT, HD), jnp.bfloat16),
            pltpu.VMEM((6 * FT, HD), jnp.bfloat16),
            pltpu.VMEM((6 * FT, 2 * HD), jnp.bfloat16),
            pltpu.VMEM((4 * FT, 2 * HD), jnp.float32),
            pltpu.VMEM((4 * FT, HD), jnp.float32),
            pltpu.VMEM((FT, FT), jnp.float32),
            pltpu.VMEM((FT, FT), jnp.float32),
            pltpu.VMEM((FT, HD), jnp.float32),
            pltpu.VMEM((FT, HD), jnp.float32),
            pltpu.VMEM((16, 8, HD), jnp.float32),
            pltpu.VMEM((4, 8, HD), jnp.float32),
            pltpu.VMEM((2 * FT, HD), jnp.bfloat16),
            pltpu.VMEM((2 * FT, HD), jnp.bfloat16),
            pltpu.VMEM((12, 8, HD), jnp.float32),
            pltpu.VMEM((2 * FT, HD), jnp.bfloat16),
            pltpu.VMEM((12, 8, HD), jnp.float32),
            pltpu.VMEM((8, BLK, HD), jnp.bfloat16),
            pltpu.SemaphoreType.DMA((6,)),
            pltpu.SemaphoreType.DMA((49,)),
            pltpu.SemaphoreType.DMA((29,)),
        ],
        compiler_params=pltpu.CompilerParams(
            collective_id=0, has_side_effects=True, vmem_limit_bytes=36000000),
        name="attend",
    )(query_states, key_states, value_states, win_start, group_end)
    return jnp.dot(rows, out_weight, preferred_element_type=jnp.float32).astype(jnp.bfloat16)


def solution(mesh):
    in_specs = (P("tm", "head"), P("tm", "head"), P("tm", "head"), P("tm"), P("tm"), P())
    out_specs = P(("tm", "head"), None)
    return jax.shard_map(local, mesh=mesh, in_specs=in_specs, out_specs=out_specs, check_vma=False)
```

```python
import jax
import jax.numpy as jnp
from jax import lax
from jax.experimental import pallas as pl
from jax.experimental.pallas import tpu as pltpu
from jax.sharding import PartitionSpec as P

HD = 128
FT = 768
BLK = 192
C = HD**-0.5 * 1.4426950408889634
HIDE = -1.0e6
LOW = -3.0e6
MESH = pl.DeviceIdType.MESH

Q0 = (0, 1, 2, 2, 0, 3, 1, 0, 1, 0, 1)
K0 = (0, 0, 1, 2, 1, 2, 1, 4, 4, 5, 5)
Q1 = (0, 1, 0, 1, 0, 1, 0, 1, 1, 0, 0)
K1 = (0, 0, 1, 1, 2, 2, 3, 3, 5, 5, 4)

PK0, PV0, PK1, PV1, TK, TV, RQ0, RQ1, RB, RO, RT, SK, SV, RH = (
    0, 1, 2, 3, 4, 5, 6, 7, 8, 9, 11, 13, 17, 21)
S1S, S2S, S3S, S4S, SH = 13, 21, 27, 33, 41


def kernel(q_hbm, k_hbm, v_hbm, ws_hbm, ge_hbm, out_ref, ws, ge, qb, kb, vb, acc, mm, s0, s1, x0, x1,
           bt, bs, att, ro, rs, reto, rets, gath, lsem, ssem, rsem, gate):
    tm = lax.axis_index("tm")
    hd = lax.axis_index("head")
    core = lax.rem(tm, 2)
    c = lax.div(tm, 2)
    x = lax.div(c, 4)
    zh = lax.rem(c, 4)
    other = tm + 1 - 2 * core
    has_prev = c > 0
    has_next = c < 15
    first = (c == 0).astype(jnp.int32)
    last = (c == 15).astype(jnp.int32)
    is0 = core == 0
    is1 = core == 1

    def both(*conds):
        r = conds[0]
        for d in conds[1:]:
            r = jnp.logical_and(r, d)
        return r

    def rc(src, dst, si, ri, t, h):
        return pltpu.make_async_remote_copy(
            src_ref=src, dst_ref=dst, send_sem=ssem.at[si], recv_sem=rsem.at[ri],
            device_id=(t, h), device_id_type=MESH)

    def got(dst, ri):
        rc(dst, dst, 0, ri, other, hd).wait_recv()

    def sent(src, si):
        rc(src, src, si, 0, other, hd).wait_send()

    def kf(n):
        return kb.at[pl.ds(n * FT, FT)]

    def vf(n):
        return vb.at[pl.ds(n * FT, FT), pl.ds(0, HD)]

    def kp(p):
        return kb.at[pl.ds(pl.multiple_of(5 * FT + p * BLK, BLK), BLK)]

    def vp(p):
        return vb.at[pl.ds(pl.multiple_of(5 * FT + p * BLK, BLK), BLK), pl.ds(0, HD)]

    barrier = pltpu.get_barrier_semaphore()

    def hello(t, h):
        pl.semaphore_signal(barrier, inc=1, device_id=(t, h), device_id_type=MESH)

    own = (
        pltpu.make_async_copy(q_hbm, qb.at[pl.ds(0, 2 * FT)], lsem.at[0]),
        pltpu.make_async_copy(k_hbm, kb.at[pl.ds(0, 2 * FT)], lsem.at[1]),
        pltpu.make_async_copy(v_hbm, vb.at[pl.ds(0, 2 * FT), pl.ds(0, HD)], lsem.at[2]),
    )
    for cp in own:
        cp.start()
    limits = (pltpu.make_async_copy(ws_hbm, ws, lsem.at[4]), pltpu.make_async_copy(ge_hbm, ge, lsem.at[5]))
    for cp in limits:
        cp.start()

    vb[:, HD:] = jnp.ones((6 * FT, HD), jnp.bfloat16)

    hello(other, hd)
    for d in range(1, 8):
        hello(tm, lax.rem(hd + d, 8))
    @pl.when(is1)
    def _():
        for d in range(1, 4):
            hello(2 * (lax.rem(x + d, 4) * 4 + zh) + 1, hd)

    @pl.when(both(is0, has_prev))
    def _():
        hello(tm - 2, hd)
        hello(tm - 1, hd)

    @pl.when(both(is0, has_next))
    def _():
        hello(tm + 2, hd)

    via = jnp.logical_and(x == 3, zh == 2)

    @pl.when(both(is1, zh > 0))
    def _():
        hello(8 * x + 1 + 6 * via.astype(jnp.int32), hd)

    @pl.when(both(is1, zh == 0, x > 0))
    def _():
        hello(0, hd)

    root = both(is0, c == 0)

    def bias(slot, frame):
        seen = jnp.logical_and(frame >= 1, jnp.logical_and(frame >= ws[slot], frame <= ge[slot]))
        return jnp.full((8, HD), jnp.where(seen, 0.0, HIDE), jnp.float32)

    for cp in limits:
        cp.wait()
    base = 2 * tm
    part = 2 * other
    for s in range(2):
        bt[s * 6 + 0] = bias(s, base)
        bt[s * 6 + 1] = bias(s, base + 1)
        bt[s * 6 + 2] = bias(s, part)
        bt[s * 6 + 3] = bias(s, part + 1)
        bt[s * 6 + 4] = bias(s, 4 * c - 1)
        bt[s * 6 + 5] = jnp.zeros((8, HD), jnp.float32)
    for s in range(2):
        for m in range(2):
            bs[2 * s + m] = bias(s, 4 * c - 3 + m)

    edge = lax.div(x, 3)
    low = (3 - edge) * (zh == 0).astype(jnp.int32) + edge * lax.div(zh, 3)
    pl.semaphore_wait(barrier, 8 + (1 - core) * (2 - last - first + 3 * first) + core * (3 + low + 1 - last))

    par = [
        rc(k_hbm.at[pl.ds(0, FT)], kf(2), PK0, PK0, other, hd),
        rc(v_hbm.at[pl.ds(0, FT)], vf(2), PV0, PV0, other, hd),
        rc(k_hbm.at[pl.ds(FT, FT)], kf(3), PK1, PK1, other, hd),
        rc(v_hbm.at[pl.ds(FT, FT)], vf(3), PV1, PV1, other, hd),
    ]
    send_q = [
        rc(q_hbm.at[pl.ds(0, FT)], qb.at[pl.ds(2 * FT, FT)], RQ0, RQ0, tm - 2, hd),
        rc(bs, bt.at[pl.ds(12, 4)], RB, RB, tm - 2, hd),
        rc(q_hbm.at[pl.ds(FT, FT)], qb.at[pl.ds(3 * FT, FT)], RQ1, RQ1, tm - 2, hd),
    ]
    send_t = [
        rc(k_hbm.at[pl.ds(FT, FT)], kf(4), TK, TK, tm + 1, hd),
        rc(v_hbm.at[pl.ds(FT, FT)], vf(4), TV, TV, tm + 1, hd),
    ]

    @pl.when(both(is0, has_prev))
    def _():
        send_q[0].start()
        send_q[1].start()

    @pl.when(both(is1, has_next))
    def _():
        send_t[0].start()

    @pl.when(both(is1, has_next, zh > 0))
    def _():
        send_t[1].start()

    stage1 = []
    for d in range(4):
        rows = pl.ds(d * BLK, BLK)
        stage1.append(rc(k_hbm.at[rows], kp(d), S1S + 2 * d, SK + d, 8 * d + 1, hd))
        stage1.append(rc(v_hbm.at[rows], vp(d), S1S + 2 * d + 1, SV + d, 8 * d + 1, hd))

    @pl.when(root)
    def _():
        for cp in stage1:
            cp.start()

    stage2 = []
    for d in (2, 1):
        stage2.append(rc(kp(x), kp(x), S2S + 2 * d, SK + x, tm + 2 * d, hd))
        stage2.append(rc(vp(x), vp(x), S2S + 2 * d + 1, SV + x, tm + 2 * d, hd))
    stage2b = (rc(kp(x), kp(x), S2S, SK + x, tm + 6, hd), rc(vp(x), vp(x), S2S + 1, SV + x, tm + 6, hd))
    stage2c = (rc(kp(x), kp(x), S2S, SK + x, tm - 2, hd), rc(vp(x), vp(x), S2S + 1, SV + x, tm - 2, hd))
    stage3 = []
    for d in (2, 1, 3):
        t = 2 * (lax.rem(x + d, 4) * 4 + zh) + 1
        stage3.append(rc(kp(x), kp(x), S3S + 2 * d - 2, SK + x, t, hd))
        stage3.append(rc(vp(x), vp(x), S3S + 2 * d - 1, SV + x, t, hd))

    def stage4(p):
        return (rc(kp(p), kp(p), S4S + 2 * p, SK + p, other, hd), rc(vp(p), vp(p), S4S + 2 * p + 1, SV + p, other, hd))

    mm[...] = jnp.full_like(mm, LOW)
    acc[...] = jnp.zeros_like(acc)

    for cp in own:
        cp.wait()

    def pick(i, a, b):
        r = a[0] + core * (b[0] - a[0])
        for m in range(1, len(a)):
            r = jnp.where(i == m, a[m] + core * (b[m] - a[m]), r)
        return r

    def item(i):
        qs = pick(i, Q0, Q1)
        ks = pick(i, K0, K1)
        qd = qs - 2 * last * lax.div(qs, 2)
        kd = ks - 4 * first * (lax.div(ks, 4) - lax.div(ks, 5))
        far = lax.div(qs, 2)
        bi = (1 - far) * (qs * 6 + ks) + far * (12 + (qs - 2) * 2 + ks - 1)
        return (pl.multiple_of(qs * FT, FT), pl.multiple_of(qd * FT, FT),
                pl.multiple_of(kd * FT, FT), bi)

    def scores(i, s_ref, x_ref):
        _, qd, kd, bi = item(i)
        s = lax.dot_general(qb[pl.ds(qd, FT), :], kb[pl.ds(kd, FT), :],
                            (((1,), (1,)), ((), ())), preferred_element_type=jnp.float32)
        s_ref[...] = s
        t = s[:, :HD]
        for l in range(HD, FT, HD):
            t = jnp.maximum(t, s[:, l:l + HD])
        top = jnp.broadcast_to(jnp.max(t, axis=1, keepdims=True), (FT, HD))
        x_ref[...] = top + bt[bi][0:1]

    def mix(i, s_ref, x_ref):
        qs, _, kd, bi = item(i)
        rows = pl.ds(qs, FT)
        old = mm[rows, :]
        new = jnp.maximum(old, x_ref[...])
        keep = jnp.exp2((old - new) * C)
        mm[rows, :] = new
        sub = new - bt[bi][0:1]
        w = [jnp.exp2((s_ref[:, l:l + HD] - sub) * C).astype(jnp.bfloat16)
             for l in range(0, FT, HD)]
        d = jnp.dot(jnp.concatenate(w, axis=1), vb[pl.ds(kd, FT), :],
                    preferred_element_type=jnp.float32)
        acc[rows, :HD] = acc[rows, :HD] * keep + d[:, :HD]
        acc[rows, HD:] = acc[rows, HD:] * keep + d[:, HD:]

    eye = (lax.broadcasted_iota(jnp.int32, (HD, HD), 0)
           == lax.broadcasted_iota(jnp.int32, (HD, HD), 1))

    def give_back(s):
        def body(b, carry):
            r = pl.multiple_of((2 + s) * FT + b * HD, HD)
            o = pl.multiple_of(s * FT + b * HD, HD)
            den = acc[pl.ds(r, HD), HD:]
            ro[pl.ds(o, HD), :] = (acc[pl.ds(r, HD), :HD] / den).astype(jnp.bfloat16)
            lse = mm[pl.ds(r, HD), :] + jnp.log2(den) * (1.0 / C)
            rs[s * 6 + b] = jnp.broadcast_to(
                jnp.sum(jnp.where(eye, lse, 0.0), axis=0, keepdims=True), (8, HD))
            return carry

        lax.fori_loop(0, 6, body, 0)

    def returns(s):
        return (rc(ro.at[pl.ds(s * FT, FT)], reto.at[pl.ds(s * FT, FT)], RO + s, RO + s, tm + 2, hd),
                rc(rs.at[pl.ds(s * 6, 6)], rets.at[pl.ds(s * 6, 6)], RT + s, RT + s, tm + 2, hd))

    relay = (rc(kf(4), kf(4), TK, TK, other, hd), rc(vf(4), vf(4), TV, TV, other, hd))

    def finish(s):
        merged = both(is0, has_prev)

        @pl.when(merged)
        def _():
            got(reto.at[pl.ds(s * FT, FT)], RO + s)
            got(rets.at[pl.ds(s * 6, 6)], RT + s)

            def body(b, carry):
                r = pl.multiple_of(s * FT + b * HD, HD)
                row = jnp.broadcast_to(rets[s * 6 + b][0:1], (HD, HD))
                far = jnp.broadcast_to(
                    jnp.sum(jnp.where(eye, row, 0.0), axis=1, keepdims=True), (HD, HD))
                old = mm[pl.ds(r, HD), :]
                new = jnp.maximum(old, far)
                a = jnp.exp2((old - new) * C)
                b2 = jnp.exp2((far - new) * C)
                num = acc[pl.ds(r, HD), :HD] * a + reto[pl.ds(r, HD), :].astype(jnp.float32) * b2
                den = acc[pl.ds(r, HD), HD:] * a + b2
                att[pl.ds(r, HD), :] = (num / den).astype(jnp.bfloat16)
                return carry

            lax.fori_loop(0, 6, body, 0)

        @pl.when(jnp.logical_not(merged))
        def _():
            def body(b, carry):
                r = pl.multiple_of(s * FT + b * HD, HD)
                att[pl.ds(r, HD), :] = (acc[pl.ds(r, HD), :HD] / acc[pl.ds(r, HD), HD:]).astype(jnp.bfloat16)
                return carry

            lax.fori_loop(0, 6, body, 0)

    def block(j):
        return rc(att.at[pl.ds(pl.multiple_of(j * BLK, BLK), BLK)], gath.at[hd], SH + j, RH + hd, tm, j)

    def deliver(s):
        finish(s)
        for d in (2, 1, 3, 0):
            j = 4 * s + lax.rem(hd + d, 4)

            @pl.when(j != hd)
            def _():
                block(j).start()

            @pl.when(j == hd)
            def _():
                gath[hd] = att[pl.ds(pl.multiple_of(j * BLK, BLK), BLK), :]

    def before(i):
        @pl.when(both(is0, has_prev, i == 1))
        def _():
            send_q[2].start()

        @pl.when(i == 1 + 2 * core)
        def _():
            for cp in par[:2]:
                cp.start()

        @pl.when(both(is1, zh == 0, i == 3))
        def _():
            got(kp(x), SK + x)
            got(vp(x), SV + x)
            for cp in stage2[2:]:
                cp.start()

            @pl.when(has_next)
            def _():
                send_t[1].start()

        @pl.when(both(is0, i == 2))
        def _():
            for cp in par[2:]:
                cp.start()

            @pl.when(has_next)
            def _():
                got(qb.at[pl.ds(2 * FT, FT)], RQ0)
                got(bt.at[pl.ds(12, 4)], RB)

        @pl.when(i == 3 + core)
        def _():
            got(kf(2), PK0)
            got(vf(2), PV0)

        @pl.when(both(is0, has_next, i == 5))
        def _():
            give_back(0)
            for cp in returns(0):
                cp.start()
            got(qb.at[pl.ds(3 * FT, FT)], RQ1)

        @pl.when(both(is0, has_next, i == 7))
        def _():
            give_back(1)
            for cp in returns(1):
                cp.start()

        @pl.when(both(is1, zh == 0, x < 3, i == 7))
        def _():
            for cp in stage2[:2]:
                cp.start()

        @pl.when(both(is1, i == 6))
        def _():
            got(kf(3), PK1)
            got(vf(3), PV1)

        @pl.when(both(is0, has_prev, i == 7))
        def _():
            got(kf(4), TK)
            got(vf(4), TV)
            for cp in relay:
                cp.start()

        @pl.when(both(is1, i == 8))
        def _():
            @pl.when(zh > 0)
            def _():
                got(kp(x), SK + x)
                got(vp(x), SV + x)

            @pl.when(both(zh == 3, x == 3))
            def _():
                for cp in stage2c:
                    cp.start()

            for cp in stage3:
                cp.start()

            @pl.when(zh == 0)
            def _():
                for cp in stage2b:
                    cp.start()

            for d in range(4):
                p = lax.rem(x + d, 4)
                if d:
                    got(kp(p), SK + p)
                    got(vp(p), SV + p)
                for cp in stage4(p):
                    cp.start()

        @pl.when(both(is0, i == 9))
        def _():
            for p in range(4):
                got(kp(p), SK + p)
                got(vp(p), SV + p)

        @pl.when(both(is1, has_prev, i == 10))
        def _():
            got(kf(4), TK)
            got(vf(4), TV)

    scores(0, s0, x0)

    def step(h, carry):
        i = 2 * h
        before(i + 1)
        scores(i + 1, s1, x1)
        mix(i, s0, x0)
        before(i + 2)
        scores(i + 2, s0, x0)
        mix(i + 1, s1, x1)
        return carry

    lax.fori_loop(0, 5, step, 0)
    mix(10, s0, x0)

    deliver(0)

    @pl.when(both(is0, has_next, hd < 4))
    def _():
        for cp in returns(1):
            cp.wait_send()
        pl.semaphore_signal(gate, inc=1, device_id=(other, hd), device_id_type=MESH)

    @pl.when(both(is1, has_next, hd < 4))
    def _():
        pl.semaphore_wait(gate, 1)

    deliver(1)

    for e in range(8):
        @pl.when(e != hd)
        def _():
            got(gath.at[e], RH + e)
        out_ref[:, e * HD:(e + 1) * HD] = gath[e]

    for cp in par[:2]:
        cp.wait_send()

    @pl.when(is0)
    def _():
        for cp in par[2:]:
            cp.wait_send()

    @pl.when(is1)
    def _():
        for cp in stage3:
            cp.wait_send()
        for p in range(4):
            for cp in stage4(p):
                cp.wait_send()

    @pl.when(both(is1, zh == 0))
    def _():
        for cp in stage2[2:]:
            cp.wait_send()
        for cp in stage2b:
            cp.wait_send()

    @pl.when(both(is1, zh == 0, x < 3))
    def _():
        for cp in stage2[:2]:
            cp.wait_send()

    @pl.when(both(is1, zh == 3, x == 3))
    def _():
        for cp in stage2c:
            cp.wait_send()

    @pl.when(both(is0, has_prev))
    def _():
        for cp in send_q:
            cp.wait_send()
        for cp in relay:
            cp.wait_send()

    @pl.when(both(is0, has_next))
    def _():
        for cp in returns(0):
            cp.wait_send()

    @pl.when(both(is0, has_next, hd >= 4))
    def _():
        for cp in returns(1):
            cp.wait_send()

    @pl.when(both(is1, has_next))
    def _():
        for cp in send_t:
            cp.wait_send()

    @pl.when(root)
    def _():
        for cp in stage1:
            cp.wait_send()

    for j in range(8):
        @pl.when(j != hd)
        def _():
            block(j).wait_send()


def local(query_states, key_states, value_states, win_start, group_end, out_weight):
    query_states, key_states, value_states, win_start, group_end = (
        pltpu.with_memory_space_constraint(a, pltpu.HBM)
        for a in (query_states, key_states, value_states, win_start, group_end))
    rows = pl.pallas_call(
        kernel,
        out_shape=jax.ShapeDtypeStruct((BLK, 8 * HD), jnp.bfloat16),
        in_specs=[pl.BlockSpec(memory_space=pltpu.HBM)] * 5,
        out_specs=pl.BlockSpec(memory_space=pltpu.VMEM),
        scratch_shapes=[
            pltpu.SMEM((2,), jnp.int32),
            pltpu.SMEM((2,), jnp.int32),
            pltpu.VMEM((4 * FT, HD), jnp.bfloat16),
            pltpu.VMEM((6 * FT, HD), jnp.bfloat16),
            pltpu.VMEM((6 * FT, 2 * HD), jnp.bfloat16),
            pltpu.VMEM((4 * FT, 2 * HD), jnp.float32),
            pltpu.VMEM((4 * FT, HD), jnp.float32),
            pltpu.VMEM((FT, FT), jnp.float32),
            pltpu.VMEM((FT, FT), jnp.float32),
            pltpu.VMEM((FT, HD), jnp.float32),
            pltpu.VMEM((FT, HD), jnp.float32),
            pltpu.VMEM((16, 8, HD), jnp.float32),
            pltpu.VMEM((4, 8, HD), jnp.float32),
            pltpu.VMEM((2 * FT, HD), jnp.bfloat16),
            pltpu.VMEM((2 * FT, HD), jnp.bfloat16),
            pltpu.VMEM((12, 8, HD), jnp.float32),
            pltpu.VMEM((2 * FT, HD), jnp.bfloat16),
            pltpu.VMEM((12, 8, HD), jnp.float32),
            pltpu.VMEM((8, BLK, HD), jnp.bfloat16),
            pltpu.SemaphoreType.DMA((6,)),
            pltpu.SemaphoreType.DMA((49,)),
            pltpu.SemaphoreType.DMA((29,)),
            pltpu.SemaphoreType.REGULAR,
        ],
        compiler_params=pltpu.CompilerParams(
            collective_id=0, has_side_effects=True, vmem_limit_bytes=36000000),
        name="attend",
    )(query_states, key_states, value_states, win_start, group_end)
    return jnp.dot(rows, out_weight, preferred_element_type=jnp.float32).astype(jnp.bfloat16)


def solution(mesh):
    in_specs = (P("tm", "head"), P("tm", "head"), P("tm", "head"), P("tm"), P("tm"), P())
    out_specs = P(("tm", "head"), None)
    return jax.shard_map(local, mesh=mesh, in_specs=in_specs, out_specs=out_specs, check_vma=False)
```

```python
import jax
import jax.numpy as jnp
from jax import lax
from jax.experimental import pallas as pl
from jax.experimental.pallas import tpu as pltpu
from jax.sharding import PartitionSpec as P

HD = 128
FT = 768
BLK = 192
C = HD**-0.5 * 1.4426950408889634
HIDE = -1.0e6
LOW = -3.0e6
MESH = pl.DeviceIdType.MESH

Q0 = (0, 1, 2, 2, 0, 3, 1, 0, 1, 0, 1)
K0 = (0, 0, 1, 2, 1, 2, 1, 4, 4, 5, 5)
Q1 = (0, 1, 0, 1, 0, 1, 0, 1, 1, 0, 0)
K1 = (0, 0, 1, 1, 2, 2, 3, 3, 5, 5, 4)

PK0, PV0, PK1, PV1, TK, TV, RQ0, RQ1, RB, RO, RT, SK, SV, RH = (
    0, 1, 2, 3, 4, 5, 6, 7, 8, 9, 11, 13, 17, 21)
S1S, S2S, S3S, S4S, SH = 13, 21, 27, 33, 41


def kernel(q_hbm, k_hbm, v_hbm, ws_hbm, ge_hbm, out_ref, ws, ge, qb, kb, vb, acc, mm, s0, s1, x0, x1,
           bt, bs, att, ro, rs, reto, rets, gath, lsem, ssem, rsem):
    tm = lax.axis_index("tm")
    hd = lax.axis_index("head")
    core = lax.rem(tm, 2)
    c = lax.div(tm, 2)
    x = lax.div(c, 4)
    zh = lax.rem(c, 4)
    other = tm + 1 - 2 * core
    has_prev = c > 0
    has_next = c < 15
    first = (c == 0).astype(jnp.int32)
    last = (c == 15).astype(jnp.int32)
    is0 = core == 0
    is1 = core == 1

    def both(*conds):
        r = conds[0]
        for d in conds[1:]:
            r = jnp.logical_and(r, d)
        return r

    def rc(src, dst, si, ri, t, h):
        return pltpu.make_async_remote_copy(
            src_ref=src, dst_ref=dst, send_sem=ssem.at[si], recv_sem=rsem.at[ri],
            device_id=(t, h), device_id_type=MESH)

    def got(dst, ri):
        rc(dst, dst, 0, ri, other, hd).wait_recv()

    def sent(src, si):
        rc(src, src, si, 0, other, hd).wait_send()

    def kf(n):
        return kb.at[pl.ds(n * FT, FT)]

    def vf(n):
        return vb.at[pl.ds(n * FT, FT), pl.ds(0, HD)]

    def kp(p):
        return kb.at[pl.ds(pl.multiple_of(5 * FT + p * BLK, BLK), BLK)]

    def vp(p):
        return vb.at[pl.ds(pl.multiple_of(5 * FT + p * BLK, BLK), BLK), pl.ds(0, HD)]

    barrier = pltpu.get_barrier_semaphore()

    def hello(t, h):
        pl.semaphore_signal(barrier, inc=1, device_id=(t, h), device_id_type=MESH)

    own = (
        pltpu.make_async_copy(q_hbm, qb.at[pl.ds(0, 2 * FT)], lsem.at[0]),
        pltpu.make_async_copy(k_hbm, kb.at[pl.ds(0, 2 * FT)], lsem.at[1]),
        pltpu.make_async_copy(v_hbm, vb.at[pl.ds(0, 2 * FT), pl.ds(0, HD)], lsem.at[2]),
    )
    for cp in own:
        cp.start()
    limits = (pltpu.make_async_copy(ws_hbm, ws, lsem.at[4]), pltpu.make_async_copy(ge_hbm, ge, lsem.at[5]))
    for cp in limits:
        cp.start()

    vb[:, HD:] = jnp.ones((6 * FT, HD), jnp.bfloat16)

    hello(other, hd)
    for d in range(1, 8):
        hello(tm, lax.rem(hd + d, 8))
    @pl.when(is1)
    def _():
        for d in range(1, 4):
            hello(2 * (lax.rem(x + d, 4) * 4 + zh) + 1, hd)

    @pl.when(both(is0, has_prev))
    def _():
        hello(tm - 2, hd)
        hello(tm - 1, hd)

    @pl.when(both(is0, has_next))
    def _():
        hello(tm + 2, hd)

    @pl.when(both(is1, zh > 0))
    def _():
        hello(tm - 2 - 4 * lax.div(zh, 3), hd)

    @pl.when(both(is1, zh == 0, x > 0))
    def _():
        hello(0, hd)

    root = both(is0, c == 0)

    def bias(slot, frame):
        seen = jnp.logical_and(frame >= 1, jnp.logical_and(frame >= ws[slot], frame <= ge[slot]))
        return jnp.full((8, HD), jnp.where(seen, 0.0, HIDE), jnp.float32)

    for cp in limits:
        cp.wait()
    base = 2 * tm
    part = 2 * other
    for s in range(2):
        bt[s * 6 + 0] = bias(s, base)
        bt[s * 6 + 1] = bias(s, base + 1)
        bt[s * 6 + 2] = bias(s, part)
        bt[s * 6 + 3] = bias(s, part + 1)
        bt[s * 6 + 4] = bias(s, 4 * c - 1)
        bt[s * 6 + 5] = jnp.zeros((8, HD), jnp.float32)
    for s in range(2):
        for m in range(2):
            bs[2 * s + m] = bias(s, 4 * c - 3 + m)

    low = 2 - zh + lax.div(zh, 3)
    pl.semaphore_wait(barrier, 8 + (1 - core) * (2 - last - first + 3 * first) + core * (3 + low + 1 - last))

    par = [
        rc(k_hbm.at[pl.ds(0, FT)], kf(2), PK0, PK0, other, hd),
        rc(v_hbm.at[pl.ds(0, FT)], vf(2), PV0, PV0, other, hd),
        rc(k_hbm.at[pl.ds(FT, FT)], kf(3), PK1, PK1, other, hd),
        rc(v_hbm.at[pl.ds(FT, FT)], vf(3), PV1, PV1, other, hd),
    ]
    send_q = [
        rc(q_hbm.at[pl.ds(0, FT)], qb.at[pl.ds(2 * FT, FT)], RQ0, RQ0, tm - 2, hd),
        rc(bs, bt.at[pl.ds(12, 4)], RB, RB, tm - 2, hd),
        rc(q_hbm.at[pl.ds(FT, FT)], qb.at[pl.ds(3 * FT, FT)], RQ1, RQ1, tm - 2, hd),
    ]
    send_t = [
        rc(k_hbm.at[pl.ds(FT, FT)], kf(4), TK, TK, tm + 1, hd),
        rc(v_hbm.at[pl.ds(FT, FT)], vf(4), TV, TV, tm + 1, hd),
    ]

    @pl.when(both(is0, has_prev))
    def _():
        send_q[0].start()
        send_q[1].start()

    @pl.when(both(is1, has_next))
    def _():
        send_t[0].start()

    @pl.when(both(is1, has_next, zh > 0))
    def _():
        send_t[1].start()

    stage1 = []
    for d in range(4):
        rows = pl.ds(d * BLK, BLK)
        stage1.append(rc(k_hbm.at[rows], kp(d), S1S + 2 * d, SK + d, 8 * d + 1, hd))
        stage1.append(rc(v_hbm.at[rows], vp(d), S1S + 2 * d + 1, SV + d, 8 * d + 1, hd))

    @pl.when(root)
    def _():
        for cp in stage1:
            cp.start()

    stage2 = (rc(kp(x), kp(x), S2S, SK + x, tm + 2, hd), rc(vp(x), vp(x), S2S + 1, SV + x, tm + 2, hd))
    stage2b = (rc(kp(x), kp(x), S2S + 2, SK + x, tm + 6, hd), rc(vp(x), vp(x), S2S + 3, SV + x, tm + 6, hd))
    stage3 = []
    for d in (2, 1, 3):
        t = 2 * (lax.rem(x + d, 4) * 4 + zh) + 1
        stage3.append(rc(kp(x), kp(x), S3S + 2 * d - 2, SK + x, t, hd))
        stage3.append(rc(vp(x), vp(x), S3S + 2 * d - 1, SV + x, t, hd))

    def stage4(p):
        return (rc(kp(p), kp(p), S4S + 2 * p, SK + p, other, hd), rc(vp(p), vp(p), S4S + 2 * p + 1, SV + p, other, hd))

    mm[...] = jnp.full_like(mm, LOW)
    acc[...] = jnp.zeros_like(acc)

    for cp in own:
        cp.wait()

    def pick(i, a, b):
        r = a[0] + core * (b[0] - a[0])
        for m in range(1, len(a)):
            r = jnp.where(i == m, a[m] + core * (b[m] - a[m]), r)
        return r

    def item(i):
        qs = pick(i, Q0, Q1)
        ks = pick(i, K0, K1)
        qd = qs - 2 * last * lax.div(qs, 2)
        kd = ks - 4 * first * (lax.div(ks, 4) - lax.div(ks, 5))
        far = lax.div(qs, 2)
        bi = (1 - far) * (qs * 6 + ks) + far * (12 + (qs - 2) * 2 + ks - 1)
        return (pl.multiple_of(qs * FT, FT), pl.multiple_of(qd * FT, FT),
                pl.multiple_of(kd * FT, FT), bi)

    def scores(i, s_ref, x_ref):
        _, qd, kd, bi = item(i)
        s = lax.dot_general(qb[pl.ds(qd, FT), :], kb[pl.ds(kd, FT), :],
                            (((1,), (1,)), ((), ())), preferred_element_type=jnp.float32)
        s_ref[...] = s
        t = s[:, :HD]
        for l in range(HD, FT, HD):
            t = jnp.maximum(t, s[:, l:l + HD])
        top = jnp.broadcast_to(jnp.max(t, axis=1, keepdims=True), (FT, HD))
        x_ref[...] = top + bt[bi][0:1]

    def mix(i, s_ref, x_ref):
        qs, _, kd, bi = item(i)
        rows = pl.ds(qs, FT)
        old = mm[rows, :]
        new = jnp.maximum(old, x_ref[...])
        keep = jnp.exp2((old - new) * C)
        mm[rows, :] = new
        sub = new - bt[bi][0:1]
        w = [jnp.exp2((s_ref[:, l:l + HD] - sub) * C).astype(jnp.bfloat16)
             for l in range(0, FT, HD)]
        d = jnp.dot(jnp.concatenate(w, axis=1), vb[pl.ds(kd, FT), :],
                    preferred_element_type=jnp.float32)
        acc[rows, :HD] = acc[rows, :HD] * keep + d[:, :HD]
        acc[rows, HD:] = acc[rows, HD:] * keep + d[:, HD:]

    eye = (lax.broadcasted_iota(jnp.int32, (HD, HD), 0)
           == lax.broadcasted_iota(jnp.int32, (HD, HD), 1))

    def give_back(s):
        def body(b, carry):
            r = pl.multiple_of((2 + s) * FT + b * HD, HD)
            o = pl.multiple_of(s * FT + b * HD, HD)
            den = acc[pl.ds(r, HD), HD:]
            ro[pl.ds(o, HD), :] = (acc[pl.ds(r, HD), :HD] / den).astype(jnp.bfloat16)
            lse = mm[pl.ds(r, HD), :] + jnp.log2(den) * (1.0 / C)
            rs[s * 6 + b] = jnp.broadcast_to(
                jnp.sum(jnp.where(eye, lse, 0.0), axis=0, keepdims=True), (8, HD))
            return carry

        lax.fori_loop(0, 6, body, 0)

    def returns(s):
        return (rc(ro.at[pl.ds(s * FT, FT)], reto.at[pl.ds(s * FT, FT)], RO + s, RO + s, tm + 2, hd),
                rc(rs.at[pl.ds(s * 6, 6)], rets.at[pl.ds(s * 6, 6)], RT + s, RT + s, tm + 2, hd))

    relay = (rc(kf(4), kf(4), TK, TK, other, hd), rc(vf(4), vf(4), TV, TV, other, hd))

    def finish(s):
        merged = both(is0, has_prev)

        @pl.when(merged)
        def _():
            got(reto.at[pl.ds(s * FT, FT)], RO + s)
            got(rets.at[pl.ds(s * 6, 6)], RT + s)

            def body(b, carry):
                r = pl.multiple_of(s * FT + b * HD, HD)
                row = jnp.broadcast_to(rets[s * 6 + b][0:1], (HD, HD))
                far = jnp.broadcast_to(
                    jnp.sum(jnp.where(eye, row, 0.0), axis=1, keepdims=True), (HD, HD))
                old = mm[pl.ds(r, HD), :]
                new = jnp.maximum(old, far)
                a = jnp.exp2((old - new) * C)
                b2 = jnp.exp2((far - new) * C)
                num = acc[pl.ds(r, HD), :HD] * a + reto[pl.ds(r, HD), :].astype(jnp.float32) * b2
                den = acc[pl.ds(r, HD), HD:] * a + b2
                att[pl.ds(r, HD), :] = (num / den).astype(jnp.bfloat16)
                return carry

            lax.fori_loop(0, 6, body, 0)

        @pl.when(jnp.logical_not(merged))
        def _():
            def body(b, carry):
                r = pl.multiple_of(s * FT + b * HD, HD)
                att[pl.ds(r, HD), :] = (acc[pl.ds(r, HD), :HD] / acc[pl.ds(r, HD), HD:]).astype(jnp.bfloat16)
                return carry

            lax.fori_loop(0, 6, body, 0)

    def block(j):
        return rc(att.at[pl.ds(pl.multiple_of(j * BLK, BLK), BLK)], gath.at[hd], SH + j, RH + hd, tm, j)

    def deliver(s):
        finish(s)
        for d in (2, 1, 3, 0):
            j = 4 * s + lax.rem(hd + d, 4)

            @pl.when(j != hd)
            def _():
                block(j).start()

            @pl.when(j == hd)
            def _():
                gath[hd] = att[pl.ds(pl.multiple_of(j * BLK, BLK), BLK), :]

    def before(i):
        @pl.when(both(is0, has_prev, i == 1))
        def _():
            send_q[2].start()

        @pl.when(i == 1 + 2 * core)
        def _():
            for cp in par[:2]:
                cp.start()

        @pl.when(both(is1, zh == 0, i == 3))
        def _():
            got(kp(x), SK + x)
            got(vp(x), SV + x)
            for cp in stage2:
                cp.start()

            @pl.when(has_next)
            def _():
                send_t[1].start()

        @pl.when(both(is0, i == 2))
        def _():
            for cp in par[2:]:
                cp.start()

            @pl.when(has_next)
            def _():
                got(qb.at[pl.ds(2 * FT, FT)], RQ0)
                got(bt.at[pl.ds(12, 4)], RB)

        @pl.when(i == 3 + core)
        def _():
            got(kf(2), PK0)
            got(vf(2), PV0)

        @pl.when(both(is0, has_next, i == 5))
        def _():
            give_back(0)
            for cp in returns(0):
                cp.start()
            got(qb.at[pl.ds(3 * FT, FT)], RQ1)

        @pl.when(both(is0, has_next, i == 7))
        def _():
            give_back(1)
            for cp in returns(1):
                cp.start()

        @pl.when(both(is1, i == 6))
        def _():
            got(kf(3), PK1)
            got(vf(3), PV1)

        @pl.when(both(is0, has_prev, i == 7))
        def _():
            got(kf(4), TK)
            got(vf(4), TV)
            for cp in relay:
                cp.start()

        @pl.when(both(is1, i == 8))
        def _():
            @pl.when(zh > 0)
            def _():
                got(kp(x), SK + x)
                got(vp(x), SV + x)

            @pl.when(zh == 1)
            def _():
                for cp in stage2:
                    cp.start()

            for cp in stage3:
                cp.start()

            @pl.when(zh == 0)
            def _():
                for cp in stage2b:
                    cp.start()

            for d in range(4):
                p = lax.rem(x + d, 4)
                if d:
                    got(kp(p), SK + p)
                    got(vp(p), SV + p)
                for cp in stage4(p):
                    cp.start()

        @pl.when(both(is0, i == 9))
        def _():
            for p in range(4):
                got(kp(p), SK + p)
                got(vp(p), SV + p)

        @pl.when(both(is1, has_prev, i == 10))
        def _():
            got(kf(4), TK)
            got(vf(4), TV)

    scores(0, s0, x0)

    def step(h, carry):
        i = 2 * h
        before(i + 1)
        scores(i + 1, s1, x1)
        mix(i, s0, x0)
        before(i + 2)
        scores(i + 2, s0, x0)
        mix(i + 1, s1, x1)
        return carry

    lax.fori_loop(0, 5, step, 0)
    mix(10, s0, x0)

    deliver(0)
    deliver(1)

    for e in range(8):
        @pl.when(e != hd)
        def _():
            got(gath.at[e], RH + e)
        out_ref[:, e * HD:(e + 1) * HD] = gath[e]

    for cp in par[:2]:
        cp.wait_send()

    @pl.when(is0)
    def _():
        for cp in par[2:]:
            cp.wait_send()

    @pl.when(is1)
    def _():
        for cp in stage3:
            cp.wait_send()
        for p in range(4):
            for cp in stage4(p):
                cp.wait_send()

    @pl.when(both(is1, zh < 2))
    def _():
        for cp in stage2:
            cp.wait_send()

    @pl.when(both(is1, zh == 0))
    def _():
        for cp in stage2b:
            cp.wait_send()

    @pl.when(both(is0, has_prev))
    def _():
        for cp in send_q:
            cp.wait_send()
        for cp in relay:
            cp.wait_send()

    @pl.when(both(is0, has_next))
    def _():
        for s in range(2):
            for cp in returns(s):
                cp.wait_send()

    @pl.when(both(is1, has_next))
    def _():
        for cp in send_t:
            cp.wait_send()

    @pl.when(root)
    def _():
        for cp in stage1:
            cp.wait_send()

    for j in range(8):
        @pl.when(j != hd)
        def _():
            block(j).wait_send()


def local(query_states, key_states, value_states, win_start, group_end, out_weight):
    query_states, key_states, value_states, win_start, group_end = (
        pltpu.with_memory_space_constraint(a, pltpu.HBM)
        for a in (query_states, key_states, value_states, win_start, group_end))
    rows = pl.pallas_call(
        kernel,
        out_shape=jax.ShapeDtypeStruct((BLK, 8 * HD), jnp.bfloat16),
        in_specs=[pl.BlockSpec(memory_space=pltpu.HBM)] * 5,
        out_specs=pl.BlockSpec(memory_space=pltpu.VMEM),
        scratch_shapes=[
            pltpu.SMEM((2,), jnp.int32),
            pltpu.SMEM((2,), jnp.int32),
            pltpu.VMEM((4 * FT, HD), jnp.bfloat16),
            pltpu.VMEM((6 * FT, HD), jnp.bfloat16),
            pltpu.VMEM((6 * FT, 2 * HD), jnp.bfloat16),
            pltpu.VMEM((4 * FT, 2 * HD), jnp.float32),
            pltpu.VMEM((4 * FT, HD), jnp.float32),
            pltpu.VMEM((FT, FT), jnp.float32),
            pltpu.VMEM((FT, FT), jnp.float32),
            pltpu.VMEM((FT, HD), jnp.float32),
            pltpu.VMEM((FT, HD), jnp.float32),
            pltpu.VMEM((16, 8, HD), jnp.float32),
            pltpu.VMEM((4, 8, HD), jnp.float32),
            pltpu.VMEM((2 * FT, HD), jnp.bfloat16),
            pltpu.VMEM((2 * FT, HD), jnp.bfloat16),
            pltpu.VMEM((12, 8, HD), jnp.float32),
            pltpu.VMEM((2 * FT, HD), jnp.bfloat16),
            pltpu.VMEM((12, 8, HD), jnp.float32),
            pltpu.VMEM((8, BLK, HD), jnp.bfloat16),
            pltpu.SemaphoreType.DMA((6,)),
            pltpu.SemaphoreType.DMA((49,)),
            pltpu.SemaphoreType.DMA((29,)),
        ],
        compiler_params=pltpu.CompilerParams(
            collective_id=0, has_side_effects=True, vmem_limit_bytes=36000000),
        name="attend",
    )(query_states, key_states, value_states, win_start, group_end)
    return jnp.dot(rows, out_weight, preferred_element_type=jnp.float32).astype(jnp.bfloat16)


def solution(mesh):
    in_specs = (P("tm", "head"), P("tm", "head"), P("tm", "head"), P("tm"), P("tm"), P())
    out_specs = P(("tm", "head"), None)
    return jax.shard_map(local, mesh=mesh, in_specs=in_specs, out_specs=out_specs, check_vma=False)
```
